256 devices in a mesh: dp: 16 (over y, x), cls: 16 (over z, core).
Axes of the slice: x: 4, y: 4, z: 8, core: 2. Of those that a mesh axis runs over, the one named last changes fastest.
Arguments:
- images: bfloat16 [16384, 64, 128], P(('dp', 'cls')), may hold values from -6 to 6
- references: bfloat16 [256, 64, 128], P('cls'), may hold values from -0.0625 to 0.0625
- ctf: float32 [128, 64], replicated, may hold values from -1 to 1
- class_ids: int32 [16384, 1], P(('dp', 'cls')), may hold values from 0 to 255
- rot_ids: int32 [16384], P(('dp', 'cls')), may hold values from 0 to 35
- group_ids: int32 [16384], P(('dp', 'cls')), may hold values from 0 to 127
Outputs:
- best: float32 [16384], P(('dp', 'cls'))
- assigned: float32 [16384], P(('dp', 'cls'))
- class_sums: float32 [256, 64, 128], P('cls', 'dp')
- class_weights: float32 [256, 64], P('cls', 'dp')
The draws below stay inside these ranges and needn't reach their ends.
Inputs may be any that keep to these rules, and one draw needn't show every extreme that they name: `class_ids`: every class is assigned to at least one particle.
All inputs are finite; a program needn't handle non-finite values.
Results may differ from the reference program's by a relative error of at most 0.0045.
Values may be sent and summed in bfloat16 or wider, within the bound.
A program may use at most 64 MiB of HBM per device.

```python
import math
import jax
import jax.numpy as jnp
from jax import lax

PART_DEV = 64
CYCLES = 64
MODES = 64
ROTATIONS = 36
GROUPS = 128
CLASSES = 256
PARTICLES = 16384


def place_ends(array, own_key, least, top_value):
    place = [jax.random.randint(jax.random.fold_in(own_key, axis), (), 0, length) for axis, length in enumerate(array.shape)]
    longest = array.shape.index(max(array.shape))
    beside = place[:longest] + [(place[longest] + 1) % array.shape[longest]] + place[longest + 1:]
    return array.at[tuple(place)].set(least).at[tuple(beside)].set(top_value)


def steps_of(key, shape, pieces, least, largest):
    gain = 1.0
    for axis_at, shards_of in pieces:
        steps = jax.random.uniform(jax.random.fold_in(jax.random.fold_in(key, 6), axis_at), (shards_of,), jnp.float32, least / len(pieces), largest / len(pieces))
        gain = gain * jnp.repeat(jnp.exp(steps), shape[axis_at] // shards_of).reshape((-1,) + (1,) * (len(shape) - 1 - axis_at))
    return gain


def different_ones(rng, rows, amount, top, lift):
    order = jax.random.permutation(jax.random.fold_in(rng, 1), amount)
    favour = order
    for power in range(3):
        favour = favour * favour // amount
    favour = favour * lift // amount
    lots = jax.random.randint(jax.random.fold_in(rng, 2), (rows, amount), 0, 4096) + favour
    fixed_rows = jax.random.permutation(jax.random.fold_in(rng, 3), rows)[jnp.arange(amount) % rows]
    lots = jnp.where(jnp.arange(rows)[:, None] == fixed_rows[None, :], 1 << 14, lots)
    merit = lots * amount + jnp.arange(amount)
    return lax.top_k(merit.astype(jnp.int32), top)[1].astype(jnp.int32)


def noise(own_key, extent, scale, reach, split=(), held_as=jnp.bfloat16):
    values = scale * jax.random.normal(own_key, extent, jnp.float32)
    if split:
        values = values * steps_of(own_key, extent, split, -0.22, 0.18)
    return jnp.clip(values, -reach, reach).astype(held_as)


def setup_inputs(seed: int = 0) -> dict:
    seeds = jax.random.split(jax.random.key(seed), 7)
    return {
        "images": noise(seeds[0], (PARTICLES, CYCLES, 2 * MODES), 1.0, 6.0, ((0, 256),)),
        "references": noise(seeds[1], (CLASSES, CYCLES, 2 * MODES), (2 * CYCLES * MODES) ** -0.5, 0.0625, ((0, 16),)),
        "ctf": jnp.clip(jax.random.uniform(seeds[2], (GROUPS, CYCLES), jnp.float32, -1.0, 1.0), -1.0, 1.0),
        "class_ids": different_ones(seeds[3], PARTICLES, CLASSES, 1, 64),
        "rot_ids": place_ends(jax.random.randint(seeds[4], (PARTICLES,), 0, ROTATIONS), jax.random.fold_in(seeds[4], 1), 0, ROTATIONS - 1).astype(jnp.int32),
        "group_ids": place_ends(jax.random.randint(seeds[5], (PARTICLES,), 0, GROUPS), jax.random.fold_in(seeds[5], 1), 0, GROUPS - 1).astype(jnp.int32),
    }


def phase_table(modes, count):
    order = jnp.arange(modes, dtype=jnp.int32)[:, None] * jnp.arange(count, dtype=jnp.int32)[None, :]
    angle = (order % count).astype(jnp.float32) * (2.0 * math.pi / count)
    return jnp.concatenate([jnp.cos(angle), -jnp.sin(angle)], axis=0).astype(jnp.bfloat16)


def turn(images, ctf_rows, rot_ids, modes, count):
    order = (jnp.arange(modes, dtype=jnp.int32)[None, :] * rot_ids[:, None]) % count
    angle = order.astype(jnp.float32) * (2.0 * math.pi / count)
    cosine = jnp.cos(angle)[:, None, :]
    sine = jnp.sin(angle)[:, None, :]
    real = images[..., :modes].astype(jnp.float32)
    imag = images[..., modes:].astype(jnp.float32)
    weight = ctf_rows[:, :, None]
    return jnp.concatenate([weight * (real * cosine - imag * sine), weight * (real * sine + imag * cosine)], axis=2).astype(jnp.bfloat16)


def reference(images, references, ctf, class_ids, rot_ids, group_ids):
    total, cycles, width = images.shape
    modes = width // 2
    count = references.shape[0]
    phases = phase_table(modes, ROTATIONS).astype(jnp.float32)
    highest = lax.Precision.HIGHEST
    real = references[..., :modes]
    imag = references[..., modes:]
    paired = jnp.concatenate([jnp.concatenate([real, imag], axis=1), jnp.concatenate([imag, -real], axis=1)], axis=0).astype(jnp.float32)
    blocks = total // PART_DEV
    xs = (images.reshape(blocks, PART_DEV, cycles, width), class_ids[:, 0].reshape(blocks, PART_DEV),
          rot_ids.reshape(blocks, PART_DEV), group_ids.reshape(blocks, PART_DEV))

    def step(carry, item):
        sums, weights = carry
        image, classes, turns, groups = item
        ctf_rows = ctf[groups]
        weighted = (ctf_rows[:, :, None] * image.astype(jnp.float32)).astype(jnp.bfloat16)
        stacked = jnp.concatenate([weighted[..., :modes], weighted[..., modes:]], axis=1).astype(jnp.float32)
        both = jnp.einsum('ikm,ckm->icm', stacked, paired, precision=highest)
        cross = jnp.concatenate([both[:, :count], both[:, count:]], axis=2).astype(jnp.bfloat16).astype(jnp.float32)
        scores = jnp.einsum('icj,jr->icr', cross, phases, precision=highest)
        best = jnp.max(scores, axis=(1, 2))
        hit = (classes[:, None, None] == jnp.arange(count, dtype=jnp.int32)[None, :, None]) & (turns[:, None, None] == jnp.arange(ROTATIONS, dtype=jnp.int32)[None, None, :])
        picked = jnp.sum(jnp.where(hit, scores, jnp.float32(0.0)), axis=(1, 2))
        turned = turn(image, ctf_rows, turns, modes, ROTATIONS)
        hot = (classes[:, None] == jnp.arange(count, dtype=jnp.int32)[None, :])
        sums = sums + jnp.dot(hot.astype(jnp.bfloat16).T, turned.reshape(PART_DEV, -1), preferred_element_type=jnp.float32).reshape(count, cycles, width)
        weights = weights + jnp.dot(hot.astype(jnp.float32).T, ctf_rows * ctf_rows, precision=highest)
        return (sums, weights), (best, picked)

    start = (jnp.zeros((count, cycles, width), jnp.float32), jnp.zeros((count, cycles), jnp.float32))
    (sums, weights), (best, picked) = lax.scan(step, start, xs)
    return best.reshape(-1), picked.reshape(-1), sums, weights
```

```python
import functools
import math

import jax
import jax.numpy as jnp
import numpy as np
from jax import lax
from jax.experimental import pallas as pl
from jax.experimental.pallas import tpu as pltpu
from jax.sharding import PartitionSpec as P

ROT = 36
HALF = ROT // 2
QUART = ROT // 4
CORES = 2
F32 = jnp.float32
BF16 = jnp.bfloat16
I32 = jnp.int32
MESH = pl.DeviceIdType.MESH
HIGHEST = lax.Precision.HIGHEST


def bf16_value(x):
    return float(np.float32(x).astype(BF16))


def turn_table(modes):
    order = (np.arange(ROT)[:, None] * np.arange(modes)[None, :]) % ROT
    angle = order * (2.0 * math.pi / ROT)
    cos, sin = np.cos(angle), np.sin(angle)
    table = np.zeros((64, 4 * modes), np.float32)
    table[:ROT] = np.concatenate([cos, cos, -sin, sin], axis=1)
    return table


def weighted_sum(terms):
    groups = {}
    for coefficient, value in terms:
        size = round(abs(coefficient), 12)
        if size < 1e-9:
            continue
        groups.setdefault(size, []).append((coefficient > 0, value))
    total = None
    for size, members in groups.items():
        part = None
        for positive, value in members:
            if part is None:
                part = value if positive else -value
            else:
                part = part + value if positive else part - value
        if size != 1.0:
            part = part * F32(bf16_value(size))
        total = part if total is None else total + part
    return total


def rotation_scores(re, im, modes):
    fold_re, fold_im = [None] * ROT, [None] * ROT
    for m in range(modes):
        for fold, part in ((fold_re, re), (fold_im, im)):
            at = m % ROT
            fold[at] = part(m) if fold[at] is None else fold[at] + part(m)
    even = [None] * (HALF + 1)
    odd = [None] * (HALF + 1)
    even[0], even[HALF] = fold_re[0], fold_re[HALF]
    for m in range(1, HALF):
        even[m] = fold_re[m] + fold_re[ROT - m]
        odd[m] = fold_im[m] - fold_im[ROT - m]
    scores = {}
    for r in range(QUART + 1):
        cos = lambda m: math.cos(2.0 * math.pi * ((m * r) % ROT) / ROT)
        sin = lambda m: math.sin(2.0 * math.pi * ((m * r) % ROT) / ROT)
        ce = weighted_sum([(cos(m), even[m]) for m in range(0, HALF + 1, 2)])
        co = weighted_sum([(cos(m), even[m]) for m in range(1, HALF + 1, 2)])
        se = weighted_sum([(sin(m), odd[m]) for m in range(2, HALF, 2)])
        so = weighted_sum([(sin(m), odd[m]) for m in range(1, HALF, 2)])
        if r == 0:
            scores[0], scores[HALF] = ce + co, ce - co
        elif r == QUART:
            scores[r], scores[ROT - r] = ce - so, ce + so
        else:
            plus, minus, both, apart = ce + co, ce - co, se + so, se - so
            scores[r], scores[ROT - r] = plus - both, plus + both
            scores[HALF - r], scores[HALF + r] = minus + apart, minus - apart
    return scores


def kernel(
    dims,
    tab_ref, img_ref, refs_ref, ctft_ref, cid_ref, rid_ref, gid_ref,
    best_ref, asg_ref, sums_ref, wts_ref,
    img_rx, ids_tx, ids_rx, xs, s2, rhs, s3, slots, xm, cts, tail, a_tx, a_rx,
    hot, wrow, facc, wacc, p_tx, p_rx, r_tx, r_rx, fin, finw, best_acc, asg_acc, e_tx, e_rx,
    ag_s, ag_r, aa_s, aa_r, rs_s, rs_r, one_s, one_r,
):
    ny, nx, nz, pd, cy, modes, cd = dims
    ndp, width, ncls = ny * nx, 2 * modes, nz * CORES * cd
    kd = cy // ndp
    hops, half = nz // 2, modes // 2
    rows = kd * pd
    dp, cls = lax.axis_index("dp"), lax.axis_index("cls")
    z, core = cls // CORES, cls % CORES
    y, x = dp // nx, dp % nx
    partner = (dp, z * CORES + 1 - core)

    def z_peer(step):
        return (dp, ((z + step + nz) % nz) * CORES + core)

    def dp_peer(step):
        return ((y + step // nx) % ny) * nx + (x + step % nx) % nx

    def remote(src, dst, send, recv, device):
        return pltpu.make_async_remote_copy(
            src_ref=src, dst_ref=dst, send_sem=send, recv_sem=recv, device_id=device, device_id_type=MESH
        )

    barrier = pltpu.get_barrier_semaphore()
    pl.semaphore_signal(barrier, inc=1, device_id=partner, device_id_type=MESH)
    for step in range(1, nz):
        pl.semaphore_signal(barrier, inc=1, device_id=z_peer(step), device_id_type=MESH)

    def greet(step, carry):
        pl.semaphore_signal(barrier, inc=1, device_id=(dp_peer(step), cls), device_id_type=MESH)
        return carry

    lax.fori_loop(1, ndp, greet, 0)

    ids_tx[...] = jnp.zeros_like(ids_tx)
    ids_tx[0:1, 0:pd] = cid_ref[...]
    ids_tx[1:2, 0:pd] = rid_ref[...]
    ids_tx[2:3, 0:pd] = gid_ref[...]
    pl.semaphore_wait(barrier, nz + ndp - 1)
    img_copy = remote(img_ref, img_rx, one_s.at[0], one_r.at[0], partner)
    ids_copy = remote(ids_tx, ids_rx, one_s.at[1], one_r.at[1], partner)

    lane_k = lax.broadcasted_iota(I32, (modes, 2 * cy), 1)

    def ref_pair(p, carry):
        both = refs_ref[pl.ds(2 * p, 2)].astype(F32).reshape(2 * cy, width)
        turned = both.T
        re, im = turned[:modes], turned[modes:]
        s3[pl.ds(pl.multiple_of(2 * p * modes, modes), modes), :] = jnp.where(lane_k < cy, re, pltpu.roll(im, cy, 1))
        s3[pl.ds(pl.multiple_of((2 * p + 1) * modes, modes), modes), :] = jnp.where(
            lane_k < cy, pltpu.roll(re, cy, 1), im
        )
        return carry

    lax.fori_loop(0, cd // 2, ref_pair, 0)

    def ag(way, hop, part):
        src = 0 if hop == 0 else 2 * hop - 1 + way
        dst = nz - 1 if hop == hops - 1 else 2 * hop + 1 + way
        span = pl.ds(part * half, half)
        return remote(
            slots.at[src, span], slots.at[dst, span], ag_s.at[way, hop, part], ag_r.at[way, hop, part],
            z_peer(1 - 2 * way),
        )

    def ag_sent(way, hop, part):
        return hop < hops - 1 or part == way

    def ref_mode(m, carry):
        slots[0, m] = s3[pl.ds(m, cd, stride=modes), :].astype(BF16)
        return carry

    for part in range(2):
        lax.fori_loop(part * half, (part + 1) * half, ref_mode, 0)
        for way in range(2):
            if ag_sent(way, 0, part):
                ag(way, 0, part).start()
    ids_copy.start()
    img_copy.start()

    def fill(base, image, groups):
        hot_g = (lax.broadcasted_iota(I32, (ctft_ref.shape[1], 2 * pd), 0) == groups).astype(F32)
        weights = jnp.dot(ctft_ref[...], hot_g, precision=HIGHEST, preferred_element_type=F32)

        def body(block, carry):
            for u in range(8):
                at = block * 8 + u
                start = pl.multiple_of((base + at) * cy, cy)
                xs[pl.ds(start, cy), :] = image[at].astype(F32) * carry[:, u : u + 1]
            return pltpu.roll(carry, 2 * pd - 8, 1)

        lax.fori_loop(0, pd // 8, body, weights)
        return weights

    cts[...] = fill(0, img_ref, ids_tx[2:3, :])

    eye = lax.broadcasted_iota(I32, (pd, 2 * pd), 0) == lax.broadcasted_iota(I32, (pd, 2 * pd), 1)
    rot_col = jnp.sum(jnp.where(eye, ids_tx[1:2, :].astype(F32), 0.0), axis=1, keepdims=True)
    rot_hot = (lax.broadcasted_iota(I32, (pd, 64), 1).astype(F32) == rot_col).astype(F32)
    table = jnp.dot(rot_hot, tab_ref[...], precision=HIGHEST, preferred_element_type=F32)
    cosine, sine = table[:, :width], table[:, width:]
    tail[...] = jnp.zeros_like(tail)
    lane_p = lax.broadcasted_iota(I32, (1, 2 * pd), 1)
    tail[2 * kd : 2 * kd + 1, :] = jnp.where(lane_p < pd, ids_tx[0:1, :].astype(F32), 0.0)

    def turn_to(step, target):
        first = dp_peer(step) * kd
        for k in range(kd):
            row = xs[pl.ds(first + k, pd, stride=cy), :]
            spun = row * cosine + pltpu.roll(row, modes, 1) * sine
            target[step, k * pd : (k + 1) * pd, :] = spun.astype(BF16)
            weight = cts[pl.ds(first + k, 1), :]
            square = jnp.where(lane_p < pd, weight * weight, 0.0)
            high = square.astype(BF16).astype(F32)
            tail[k : k + 1, :] = high
            tail[kd + k : kd + k + 1, :] = square - high
        target[step, rows : rows + 16, :] = tail[...].astype(BF16)

    def a2a(step):
        return remote(a_tx.at[step], a_rx.at[step], aa_s.at[step], aa_r.at[step], (dp_peer(step), cls))

    def send_turned(step, carry):
        turn_to(step, a_tx)
        a2a(step).start()
        return carry

    lax.fori_loop(1, ndp, send_turned, 0)
    turn_to(0, a_rx)

    ids_copy.wait_recv()
    img_copy.wait_recv()
    fill(pd, img_rx, ids_rx[2:3, :])

    def flip(k, carry):
        s2[pl.ds(pl.multiple_of(k * width, width), width), :] = xs[pl.ds(k, 2 * pd, stride=cy), :].T
        return carry

    lax.fori_loop(0, cy, flip, 0, unroll=2)

    def spread(m, carry):
        re = s2[pl.ds(m, cy, stride=width), :]
        im = s2[pl.ds(m + modes, cy, stride=width), :]
        rhs[m, 0:cy, 0 : 2 * pd] = re.astype(BF16)
        rhs[m, 0:cy, 2 * pd : 4 * pd] = (-im).astype(BF16)
        rhs[m, cy : 2 * cy, 0 : 2 * pd] = im.astype(BF16)
        rhs[m, cy : 2 * cy, 2 * pd : 4 * pd] = re.astype(BF16)
        return carry

    lax.fori_loop(0, modes, spread, 0, unroll=2)

    lane2 = lax.broadcasted_iota(I32, (8, 2 * pd), 1)
    ids_all = jnp.where(lane2 < pd, ids_tx[...], pltpu.roll(ids_rx[...], pd, 1))
    class_row, rot_row = ids_all[0:1, :], ids_all[1:2, :]
    best_acc[...] = jnp.full_like(best_acc, -1e30)
    asg_acc[...] = jnp.zeros_like(asg_acc)
    sub8 = lax.broadcasted_iota(I32, (8, 2 * pd), 0)

    def score(first, count):
        high = count * cd

        def cross(m, carry):
            left = slots[first : first + count, m].reshape(high, 2 * cy)
            xm[m, 0:high, :] = jnp.dot(left, rhs[m], preferred_element_type=F32)
            return carry

        lax.fori_loop(0, modes, cross, 0, unroll=8)

        def column(col, carry):
            at = pl.multiple_of(col * 8, 8)
            slot = first + at // cd
            hop = (slot + 1) // 2
            source = (z + jnp.where(slot % 2 == 1, -hop, hop) + nz) % nz
            base = (source * CORES + core) * cd + at % cd
            re = lambda m: xm[m, pl.ds(at, 8), 0 : 2 * pd]
            im = lambda m: xm[m, pl.ds(at, 8), 2 * pd : 4 * pd]
            scores = rotation_scores(re, im, modes)
            top, chosen = None, jnp.zeros((8, 2 * pd), F32)
            for r, value in scores.items():
                top = value if top is None else jnp.maximum(top, value)
                chosen = jnp.where(rot_row == r, value, chosen)
            best_acc[...] = jnp.maximum(best_acc[...], top)
            asg_acc[...] = asg_acc[...] + jnp.where(class_row == base + sub8, chosen, 0.0)
            return carry

        lax.fori_loop(0, high // 8, column, 0)

    done = 0
    for hop in range(1, hops):
        for part in range(2):
            for way in range(2):
                if ag_sent(way, hop, part):
                    ag(way, hop - 1, part).wait_recv()
                    ag(way, hop, part).start()
                elif hop < hops - 1:
                    ag(way, hop - 1, part).wait_recv()
        if hop < hops - 1:
            score(done, 2 * hop + 1 - done)
            done = 2 * hop + 1

    def arrived(step, carry):
        a2a(step).wait_recv()
        return carry

    lax.fori_loop(1, ndp, arrived, 0)
    class_iota = lax.broadcasted_iota(I32, (ncls, 2 * pd), 0).astype(F32)
    for q in range(ndp // 2):
        near = a_rx[2 * q, rows : rows + 16, :].astype(F32)
        far = a_rx[2 * q + 1, rows : rows + 16, :].astype(F32)
        both = near + pltpu.roll(far, pd, 1)
        hot[:, q * 2 * pd : (q + 1) * 2 * pd] = (class_iota == both[2 * kd : 2 * kd + 1, :]).astype(F32).astype(BF16)
        wrow[:, q * 2 * pd : (q + 1) * 2 * pd] = both.astype(BF16)

    def sum_cycle(k, carry):
        right = a_rx[:, pl.ds(pl.multiple_of(k * pd, pd), pd), :].reshape(ndp * pd, width)
        facc[k] = jnp.dot(hot[...], right, preferred_element_type=F32)
        return carry

    lax.fori_loop(0, kd, sum_cycle, 0)
    wacc[...] = jnp.zeros_like(wacc)
    wacc[:, 0:16] = lax.dot_general(hot[...], wrow[...], (((1,), (1,)), ((), ())), preferred_element_type=F32)

    def block_of(owner):
        at = pl.ds(pl.multiple_of(owner * cd, cd), cd)
        return [facc[k, at, :] for k in range(kd)], wacc[at, :]

    def put(target, index, values, weights):
        for k in range(kd):
            target[index, k * cd : (k + 1) * cd, :] = values[k].astype(BF16)
        high = weights.astype(BF16)
        target[index, kd * cd : (kd + 1) * cd, :] = high
        target[index, (kd + 1) * cd : (kd + 2) * cd, :] = (weights - high.astype(F32)).astype(BF16)

    def take(source, index):
        values = [source[index, k * cd : (k + 1) * cd, :].astype(F32) for k in range(kd)]
        high = source[index, kd * cd : (kd + 1) * cd, :].astype(F32)
        return values, high + source[index, (kd + 1) * cd : (kd + 2) * cd, :].astype(F32)

    def pack(chip, carry):
        put(p_tx, chip, *block_of(chip * CORES + 1 - core))
        return carry

    lax.fori_loop(0, nz, pack, 0)
    p_copy = remote(p_tx, p_rx, one_s.at[2], one_r.at[2], partner)
    p_copy.start()
    p_copy.wait_recv()

    def chip_sum(step):
        chip = (z + step) % nz
        values, weights = block_of(chip * CORES + core)
        more, more_w = take(p_rx, chip)
        return [a + b for a, b in zip(values, more)], weights + more_w

    def rs(step):
        return remote(r_tx.at[step], r_rx.at[step], rs_s.at[step], rs_r.at[step], z_peer(step))

    def send_sums(step, carry):
        put(r_tx, step, *chip_sum(step))
        rs(step).start()
        return carry

    lax.fori_loop(1, nz, send_sums, 0)
    values, weights = chip_sum(0)
    for k in range(kd):
        fin[k] = values[k]
    finw[...] = weights

    for part in range(2):
        for way in range(2):
            if not ag_sent(way, hops - 1, part):
                ag(way, hops - 2, part).wait_recv()
    for way in range(2):
        ag(way, hops - 1, way).wait_recv()
    score(done, nz - done)

    e_tx[...] = jnp.zeros_like(e_tx)
    e_tx[0:1, :] = jnp.max(best_acc[...], axis=0, keepdims=True)
    e_tx[1:2, :] = jnp.sum(asg_acc[...], axis=0, keepdims=True)
    e_copy = remote(e_tx, e_rx, one_s.at[3], one_r.at[3], partner)
    e_copy.start()

    def reduced(step, carry):
        rs(step).wait_recv()
        more, more_w = take(r_rx, step)
        for k in range(kd):
            fin[k] = fin[k] + more[k]
        finw[...] = finw[...] + more_w
        return carry

    lax.fori_loop(1, nz, reduced, 0)
    for k in range(kd):
        sums_ref[:, k, :] = fin[k]
    wts_ref[...] = finw[:, 0:kd] + finw[:, kd : 2 * kd]

    e_copy.wait_recv()
    other = pltpu.roll(e_rx[...], pd, 1)
    best_ref[...] = jnp.maximum(e_tx[0:1, :], other[0:1, :])[:, 0:pd]
    asg_ref[...] = (e_tx[1:2, :] + other[1:2, :])[:, 0:pd]

    for hop in range(hops):
        for part in range(2):
            for way in range(2):
                if ag_sent(way, hop, part):
                    ag(way, hop, part).wait_send()

    def left_dp(step, carry):
        a2a(step).wait_send()
        return carry

    def left_z(step, carry):
        rs(step).wait_send()
        return carry

    lax.fori_loop(1, ndp, left_dp, 0)
    lax.fori_loop(1, nz, left_z, 0)
    for copy in (img_copy, ids_copy, p_copy, e_copy):
        copy.wait_send()


def on_device(dims, images, references, ctf, class_ids, rot_ids, group_ids):
    ny, nx, nz, pd, cy, modes, cd = dims
    ndp, width, ncls = ny * nx, 2 * modes, nz * CORES * cd
    kd = cy // ndp
    hops = nz // 2
    block = kd * pd + 16
    reduce_rows = (kd + 2) * cd
    most = max(nz - 2 * (hops - 2) - 1 if hops > 2 else nz, 3 if hops > 2 else 0) * cd
    row = lambda ids: ids.reshape(1, pd)
    vmem = pl.BlockSpec(memory_space=pltpu.VMEM)
    dma = pltpu.SemaphoreType.DMA
    best, assigned, sums, weights = pl.pallas_call(
        functools.partial(kernel, dims),
        out_shape=(
            jax.ShapeDtypeStruct((1, pd), F32),
            jax.ShapeDtypeStruct((1, pd), F32),
            jax.ShapeDtypeStruct((cd, kd, width), F32),
            jax.ShapeDtypeStruct((cd, kd), F32),
        ),
        in_specs=[vmem] * 7,
        out_specs=(vmem,) * 4,
        scratch_shapes=[
            pltpu.VMEM((pd, cy, width), BF16),
            pltpu.VMEM((8, 2 * pd), I32),
            pltpu.VMEM((8, 2 * pd), I32),
            pltpu.VMEM((2 * pd * cy, width), F32),
            pltpu.VMEM((cy * width, 2 * pd), F32),
            pltpu.VMEM((modes, 2 * cy, 4 * pd), BF16),
            pltpu.VMEM((cd * modes, 2 * cy), F32),
            pltpu.VMEM((nz, modes, cd, 2 * cy), BF16),
            pltpu.VMEM((modes, most, 4 * pd), F32),
            pltpu.VMEM((cy, 2 * pd), F32),
            pltpu.VMEM((16, 2 * pd), F32),
            pltpu.VMEM((ndp, block, width), BF16),
            pltpu.VMEM((ndp, block, width), BF16),
            pltpu.VMEM((ncls, ndp * pd), BF16),
            pltpu.VMEM((16, ndp * pd), BF16),
            pltpu.VMEM((kd, ncls, width), F32),
            pltpu.VMEM((ncls, width), F32),
            pltpu.VMEM((nz, reduce_rows, width), BF16),
            pltpu.VMEM((nz, reduce_rows, width), BF16),
            pltpu.VMEM((nz, reduce_rows, width), BF16),
            pltpu.VMEM((nz, reduce_rows, width), BF16),
            pltpu.VMEM((kd, cd, width), F32),
            pltpu.VMEM((cd, width), F32),
            pltpu.VMEM((8, 2 * pd), F32),
            pltpu.VMEM((8, 2 * pd), F32),
            pltpu.VMEM((8, 2 * pd), F32),
            pltpu.VMEM((8, 2 * pd), F32),
            dma((2, hops, 2)),
            dma((2, hops, 2)),
            dma((ndp,)),
            dma((ndp,)),
            dma((nz,)),
            dma((nz,)),
            dma((4,)),
            dma((4,)),
        ],
        compiler_params=pltpu.CompilerParams(
            collective_id=0, has_side_effects=True, vmem_limit_bytes=60 * 1024 * 1024
        ),
    )(
        jnp.asarray(turn_table(modes)), images, references, ctf.T, row(class_ids), row(rot_ids), row(group_ids)
    )
    return best.reshape(pd), assigned.reshape(pd), sums, weights


def plane(count):
    side = 1
    while side * side < count:
        side *= 2
    return count // side, side


def solution(mesh):
    ndp, ncl = mesh.shape["dp"], mesh.shape["cls"]
    ny, nx = plane(ndp)

    def step(images, references, ctf, class_ids, rot_ids, group_ids):
        pd, cy, width = images.shape
        dims = (ny, nx, ncl // CORES, pd, cy, width // 2, references.shape[0])
        return on_device(dims, images, references, ctf, class_ids, rot_ids, group_ids)

    both = P(("dp", "cls"))
    return jax.shard_map(
        step,
        mesh=mesh,
        in_specs=(P(("dp", "cls"), None, None), P("cls", None, None), P(), P(("dp", "cls"), None), both, both),
        out_specs=(both, both, P("cls", "dp", None), P("cls", "dp")),
        check_vma=False,
    )
```

```python
import functools
import math

import jax
import jax.numpy as jnp
import numpy as np
from jax import lax
from jax.experimental import pallas as pl
from jax.experimental.pallas import tpu as pltpu
from jax.sharding import PartitionSpec as P

ROT = 36
HALF = ROT // 2
QUART = ROT // 4
CORES = 2
F32 = jnp.float32
BF16 = jnp.bfloat16
I32 = jnp.int32
MESH = pl.DeviceIdType.MESH
HIGHEST = lax.Precision.HIGHEST


def bf16_value(x):
    return float(np.float32(x).astype(BF16))


def turn_table(modes):
    order = (np.arange(ROT)[:, None] * np.arange(modes)[None, :]) % ROT
    angle = order * (2.0 * math.pi / ROT)
    cos, sin = np.cos(angle), np.sin(angle)
    table = np.zeros((64, 4 * modes), np.float32)
    table[:ROT] = np.concatenate([cos, cos, -sin, sin], axis=1)
    return table


def weighted_sum(terms):
    groups = {}
    for coefficient, value in terms:
        size = round(abs(coefficient), 12)
        if size < 1e-9:
            continue
        groups.setdefault(size, []).append((coefficient > 0, value))
    total = None
    for size, members in groups.items():
        part = None
        for positive, value in members:
            if part is None:
                part = value if positive else -value
            else:
                part = part + value if positive else part - value
        if size != 1.0:
            part = part * F32(bf16_value(size))
        total = part if total is None else total + part
    return total


def rotation_scores(re, im, modes):
    fold_re, fold_im = [None] * ROT, [None] * ROT
    for m in range(modes):
        for fold, part in ((fold_re, re), (fold_im, im)):
            at = m % ROT
            fold[at] = part(m) if fold[at] is None else fold[at] + part(m)
    even = [None] * (HALF + 1)
    odd = [None] * (HALF + 1)
    even[0], even[HALF] = fold_re[0], fold_re[HALF]
    for m in range(1, HALF):
        even[m] = fold_re[m] + fold_re[ROT - m]
        odd[m] = fold_im[m] - fold_im[ROT - m]
    scores = {}
    for r in range(QUART + 1):
        cos = lambda m: math.cos(2.0 * math.pi * ((m * r) % ROT) / ROT)
        sin = lambda m: math.sin(2.0 * math.pi * ((m * r) % ROT) / ROT)
        ce = weighted_sum([(cos(m), even[m]) for m in range(0, HALF + 1, 2)])
        co = weighted_sum([(cos(m), even[m]) for m in range(1, HALF + 1, 2)])
        se = weighted_sum([(sin(m), odd[m]) for m in range(2, HALF, 2)])
        so = weighted_sum([(sin(m), odd[m]) for m in range(1, HALF, 2)])
        if r == 0:
            scores[0], scores[HALF] = ce + co, ce - co
        elif r == QUART:
            scores[r], scores[ROT - r] = ce - so, ce + so
        else:
            plus, minus, both, apart = ce + co, ce - co, se + so, se - so
            scores[r], scores[ROT - r] = plus - both, plus + both
            scores[HALF - r], scores[HALF + r] = minus + apart, minus - apart
    return scores


def kernel(
    dims,
    tab_ref, img_ref, refs_ref, ctft_ref, cid_ref, rid_ref, gid_ref,
    out_ref,
    img_rx, ids_tx, ids_rx, xs, s2, rhs, s3, slots, xm, cts, tail, a_tx, a_rx,
    hot, wrow, facc, wacc, p_tx, p_rx, r_tx, r_rx, best_acc, asg_acc, e_tx, e_rx,
    ag_s, ag_r, aa_s, aa_r, pt_s, pt_r, rs_s, rs_r, one_s, one_r,
):
    ny, nx, nz, pd, cy, modes, cd = dims
    ndp, width, ncls = ny * nx, 2 * modes, nz * CORES * cd
    kd = cy // ndp
    hops, half = nz // 2, modes // 2
    px, pk, pm = cy + 1, width + 1, modes + 1
    dp, cls = lax.axis_index("dp"), lax.axis_index("cls")
    z, core = cls // CORES, cls % CORES
    y, x = dp // nx, dp % nx
    partner = (dp, z * CORES + 1 - core)

    def z_peer(step):
        return (dp, ((z + step + nz) % nz) * CORES + core)

    def dp_peer(step):
        return ((y + step // nx) % ny) * nx + (x + step % nx) % nx

    def remote(src, dst, send, recv, device):
        return pltpu.make_async_remote_copy(
            src_ref=src, dst_ref=dst, send_sem=send, recv_sem=recv, device_id=device, device_id_type=MESH
        )

    barrier = pltpu.get_barrier_semaphore()
    pl.semaphore_signal(barrier, inc=1, device_id=partner, device_id_type=MESH)
    for step in range(1, nz):
        pl.semaphore_signal(barrier, inc=1, device_id=z_peer(step), device_id_type=MESH)

    def greet(step, carry):
        pl.semaphore_signal(barrier, inc=1, device_id=(dp_peer(step), cls), device_id_type=MESH)
        return carry

    lax.fori_loop(1, ndp, greet, 0)

    ids_tx[...] = jnp.zeros_like(ids_tx)
    ids_tx[0:1, 0:pd] = cid_ref[...]
    ids_tx[1:2, 0:pd] = rid_ref[...]
    ids_tx[2:3, 0:pd] = gid_ref[...]
    pl.semaphore_wait(barrier, nz + ndp - 1)
    img_copy = remote(img_ref, img_rx, one_s.at[0], one_r.at[0], partner)
    ids_copy = remote(ids_tx, ids_rx, one_s.at[1], one_r.at[1], partner)

    lane_k = lax.broadcasted_iota(I32, (modes, 2 * cy), 1)

    def ref_pair(p, carry):
        both = refs_ref[pl.ds(2 * p, 2)].astype(F32).reshape(2 * cy, width)
        turned = both.T
        re, im = turned[:modes], turned[modes:]
        s3[pl.ds(2 * p * pm, modes), :] = jnp.where(lane_k < cy, re, pltpu.roll(im, cy, 1))
        s3[pl.ds((2 * p + 1) * pm, modes), :] = jnp.where(
            lane_k < cy, pltpu.roll(re, cy, 1), im
        )
        return carry

    lax.fori_loop(0, cd // 2, ref_pair, 0, unroll=4)

    def ag(way, hop, part):
        src = 0 if hop == 0 else 2 * hop - 1 + way
        dst = nz - 1 if hop == hops - 1 else 2 * hop + 1 + way
        span = pl.ds(part * half, half)
        return remote(
            slots.at[src, span], slots.at[dst, span], ag_s.at[way, hop, part], ag_r.at[way, hop, part],
            z_peer(1 - 2 * way),
        )

    def ag_sent(way, hop, part):
        return hop < hops - 1 or part == way

    def ref_mode(m, carry):
        slots[0, m] = s3[pl.ds(m, cd, stride=pm), :].astype(BF16)
        return carry

    for part in range(2):
        lax.fori_loop(part * half, (part + 1) * half, ref_mode, 0, unroll=8)
        for way in range(2):
            if ag_sent(way, 0, part):
                ag(way, 0, part).start()
    ids_copy.start()
    img_copy.start()

    def fill(base, image, groups):
        hot_g = (lax.broadcasted_iota(I32, (ctft_ref.shape[1], 2 * pd), 0) == groups).astype(F32)
        weights = jnp.dot(ctft_ref[...], hot_g, precision=HIGHEST, preferred_element_type=F32)

        def body(block, carry):
            for u in range(8):
                at = block * 8 + u
                xs[pl.ds((base + at) * px, cy), :] = image[at].astype(F32) * carry[:, u : u + 1]
            return pltpu.roll(carry, 2 * pd - 8, 1)

        lax.fori_loop(0, pd // 8, body, weights)
        return weights

    cts[...] = fill(0, img_ref, ids_tx[2:3, :])

    eye = lax.broadcasted_iota(I32, (pd, 2 * pd), 0) == lax.broadcasted_iota(I32, (pd, 2 * pd), 1)
    rot_col = jnp.sum(jnp.where(eye, ids_tx[1:2, :].astype(F32), 0.0), axis=1, keepdims=True)
    rot_hot = (lax.broadcasted_iota(I32, (pd, 64), 1).astype(F32) == rot_col).astype(F32)
    table = jnp.dot(rot_hot, tab_ref[...], precision=HIGHEST, preferred_element_type=F32)
    cosine, sine = table[:, :width], table[:, width:]
    tail[...] = jnp.zeros_like(tail)
    lane_p = lax.broadcasted_iota(I32, (1, 2 * pd), 1)
    tail[2 * kd : 2 * kd + 1, :] = jnp.where(lane_p < pd, ids_tx[0:1, :].astype(F32), 0.0)

    def turn_to(k, step, target):
        cycle = dp_peer(step) * kd + k
        row = xs[pl.ds(cycle, pd, stride=px), :]
        spun = row * cosine + pltpu.roll(row, modes, 1) * sine
        target[step, 16 + k * pd : 16 + (k + 1) * pd, :] = spun.astype(BF16)
        if k == 0:
            for at in range(kd):
                weight = cts[pl.ds(cycle + at, 1), :]
                square = jnp.where(lane_p < pd, weight * weight, 0.0)
                high = square.astype(BF16).astype(F32)
                tail[at : at + 1, :] = high
                tail[kd + at : kd + at + 1, :] = square - high
            target[step, 0:16, :] = tail[...].astype(BF16)

    def a2a(k, step):
        span = pl.ds(0, 16 + pd) if k == 0 else pl.ds(16 + k * pd, pd)
        return remote(
            a_tx.at[step, span], a_rx.at[step, span], aa_s.at[k, step], aa_r.at[k, step], (dp_peer(step), cls)
        )

    for k in range(kd):

        def send_turned(step, carry):
            turn_to(k, step, a_tx)
            a2a(k, step).start()
            return carry

        lax.fori_loop(1, ndp, send_turned, 0)
        turn_to(k, 0, a_rx)

    def forward(hop, part):
        for way in range(2):
            if ag_sent(way, hop, part):
                ag(way, hop - 1, part).wait_recv()
                ag(way, hop, part).start()
            elif hop < hops - 1:
                ag(way, hop - 1, part).wait_recv()

    ids_copy.wait_recv()
    img_copy.wait_recv()
    fill(pd, img_rx, ids_rx[2:3, :])
    forward(1, 0)

    def flip(k, carry):
        s2[pl.ds(k * pk, width), :] = xs[pl.ds(k, 2 * pd, stride=px), :].T
        return carry

    lax.fori_loop(0, cy, flip, 0, unroll=4)

    def spread(m, carry):
        re = s2[pl.ds(m, cy, stride=pk), :]
        im = s2[pl.ds(m + modes, cy, stride=pk), :]
        rhs[m, 0:cy, 0 : 2 * pd] = re.astype(BF16)
        rhs[m, 0:cy, 2 * pd : 4 * pd] = (-im).astype(BF16)
        rhs[m, cy : 2 * cy, 0 : 2 * pd] = im.astype(BF16)
        rhs[m, cy : 2 * cy, 2 * pd : 4 * pd] = re.astype(BF16)
        return carry

    lax.fori_loop(0, modes, spread, 0, unroll=4)
    forward(1, 1)

    lane2 = lax.broadcasted_iota(I32, (8, 2 * pd), 1)
    ids_all = jnp.where(lane2 < pd, ids_tx[...], pltpu.roll(ids_rx[...], pd, 1))
    class_row, rot_row = ids_all[0:1, :], ids_all[1:2, :]
    best_acc[...] = jnp.full_like(best_acc, -1e30)
    asg_acc[...] = jnp.zeros_like(asg_acc)
    sub8 = lax.broadcasted_iota(I32, (8, 2 * pd), 0)

    def score(first, count):
        high = count * cd

        def cross(m, carry):
            left = slots[first : first + count, m].reshape(high, 2 * cy)
            xm[m, 0:high, :] = jnp.dot(left, rhs[m], preferred_element_type=F32)
            return carry

        lax.fori_loop(0, modes, cross, 0, unroll=32)

        def column(col, carry):
            at = pl.multiple_of(col * 8, 8)
            slot = first + at // cd
            hop = (slot + 1) // 2
            source = (z + jnp.where(slot % 2 == 1, -hop, hop) + nz) % nz
            base = (source * CORES + core) * cd + at % cd
            re = lambda m: xm[m, pl.ds(at, 8), 0 : 2 * pd]
            im = lambda m: xm[m, pl.ds(at, 8), 2 * pd : 4 * pd]
            scores = rotation_scores(re, im, modes)
            top, chosen = None, jnp.zeros((8, 2 * pd), F32)
            for r, value in scores.items():
                top = value if top is None else jnp.maximum(top, value)
                chosen = jnp.where(rot_row == r, value, chosen)
            best_acc[...] = jnp.maximum(best_acc[...], top)
            asg_acc[...] = asg_acc[...] + jnp.where(class_row == base + sub8, chosen, 0.0)
            return carry

        lax.fori_loop(0, high // 8, column, 0)

    def one_hot():
        class_iota = lax.broadcasted_iota(I32, (ncls, 2 * pd), 0).astype(F32)
        for q in range(ndp // 2):
            near = a_rx[2 * q, 0:16, :].astype(F32)
            both = near + pltpu.roll(a_rx[2 * q + 1, 0:16, :].astype(F32), pd, 1)
            at = slice(q * 2 * pd, (q + 1) * 2 * pd)
            hot[:, at] = (class_iota == both[2 * kd : 2 * kd + 1, :]).astype(F32).astype(BF16)
            wrow[:, at] = both.astype(BF16)
        wacc[...] = jnp.zeros_like(wacc)
        wacc[:, 0:16] = lax.dot_general(hot[...], wrow[...], (((1,), (1,)), ((), ())), preferred_element_type=F32)

    def tiles(k):
        return 2 * cd if k == 0 else cd

    def at_class(owner):
        return pl.ds(pl.multiple_of(owner * cd, cd), cd)

    def with_rest(weights):
        high = weights.astype(BF16).astype(F32)
        return (high + pltpu.roll(weights - high, 16, 1)).astype(BF16)

    def without_rest(block):
        block = block.astype(F32)
        return block + pltpu.roll(block, width - 16, 1)

    def to_partner(k):
        span = pl.ds(0, tiles(k))
        return remote(p_tx.at[k, :, span], p_rx.at[k, :, span], pt_s.at[k], pt_r.at[k], partner)

    def to_owner(k, step):
        span = pl.ds(0, tiles(k))
        return remote(
            r_tx.at[k, step, span], r_rx.at[k, step, span], rs_s.at[k, step], rs_r.at[k, step], z_peer(step)
        )

    def sum_cycle(k):
        def arrived(step, carry):
            a2a(k, step).wait_recv()
            return carry

        lax.fori_loop(1, ndp, arrived, 0)
        if k == 0:
            one_hot()
        right = a_rx[:, 16 + k * pd : 16 + (k + 1) * pd, :].reshape(ndp * pd, width)
        facc[k] = jnp.dot(hot[...], right, preferred_element_type=F32)

        def pack(chip, carry):
            at = at_class(chip * CORES + 1 - core)
            p_tx[k, chip, 0:cd, :] = facc[k, at, :].astype(BF16)
            if k == 0:
                p_tx[k, chip, cd : 2 * cd, :] = with_rest(wacc[at, :])
            return carry

        lax.fori_loop(0, nz, pack, 0)
        to_partner(k).start()

    def chip_cycle(k):
        to_partner(k).wait_recv()

        def chip_sum(step):
            chip = (z + step) % nz
            at = at_class(chip * CORES + core)
            values = facc[k, at, :] + p_rx[k, chip, 0:cd, :].astype(F32)
            return values, (wacc[at, :] + without_rest(p_rx[k, chip, cd : 2 * cd, :]) if k == 0 else None)

        def send_sums(step, carry):
            values, weights = chip_sum(step)
            r_tx[k, step, 0:cd, :] = values.astype(BF16)
            if k == 0:
                keep = lax.broadcasted_iota(I32, (cd, width), 1) < 16
                r_tx[k, step, cd : 2 * cd, :] = with_rest(jnp.where(keep, weights, 0.0))
            to_owner(k, step).start()
            return carry

        lax.fori_loop(1, nz, send_sums, 0)
        values, weights = chip_sum(0)
        out_ref[k * cd : (k + 1) * cd, :] = values
        if k == 0:
            out_ref[kd * cd : (kd + 1) * cd, :] = weights

    def owned_cycle(k):
        def reduced(step, carry):
            to_owner(k, step).wait_recv()
            at = slice(k * cd, (k + 1) * cd)
            out_ref[at, :] = out_ref[at, :] + r_rx[k, step, 0:cd, :].astype(F32)
            if k == 0:
                at = slice(kd * cd, (kd + 1) * cd)
                out_ref[at, :] = out_ref[at, :] + without_rest(r_rx[k, step, cd : 2 * cd, :])
            return carry

        lax.fori_loop(1, nz, reduced, 0)

    todo = []
    for k in range(kd):
        todo.append((sum_cycle, k))
        if k > 0:
            todo.append((chip_cycle, k - 1))
    todo.append((chip_cycle, kd - 1))

    def some(count):
        for _ in range(min(count, len(todo))):
            act, k = todo.pop(0)
            act(k)

    some(1)
    done = 0
    for hop in range(2, hops):
        score(done, 2 * hop - 1 - done)
        done = 2 * hop - 1
        forward(hop, 0)
        some(2)
        forward(hop, 1)

    for part in range(2):
        for way in range(2):
            if not ag_sent(way, hops - 1, part):
                ag(way, hops - 2, part).wait_recv()
    score(done, nz - 1 - done)
    some(len(todo))
    for way in range(2):
        ag(way, hops - 1, way).wait_recv()
    score(nz - 1, 1)

    e_tx[...] = jnp.zeros_like(e_tx)
    e_tx[0:1, :] = jnp.max(best_acc[...], axis=0, keepdims=True)
    e_tx[1:2, :] = jnp.sum(asg_acc[...], axis=0, keepdims=True)
    e_copy = remote(e_tx, e_rx, one_s.at[2], one_r.at[2], partner)
    e_copy.start()

    for k in range(kd):
        owned_cycle(k)

    e_copy.wait_recv()
    other = pltpu.roll(e_rx[...], pd, 1)
    low = (kd + 1) * cd
    out_ref[low : low + 1, :] = jnp.maximum(e_tx[0:1, :], other[0:1, :])
    out_ref[low + 1 : low + 2, :] = e_tx[1:2, :] + other[1:2, :]
    out_ref[low + 2 : low + 8, :] = jnp.zeros((6, width), F32)

    for hop in range(hops):
        for part in range(2):
            for way in range(2):
                if ag_sent(way, hop, part):
                    ag(way, hop, part).wait_send()

    for k in range(kd):

        def left_dp(step, carry):
            a2a(k, step).wait_send()
            return carry

        def left_z(step, carry):
            to_owner(k, step).wait_send()
            return carry

        lax.fori_loop(1, ndp, left_dp, 0)
        lax.fori_loop(1, nz, left_z, 0)
        to_partner(k).wait_send()
    for copy in (img_copy, ids_copy, e_copy):
        copy.wait_send()


def deliver(pd, cd, kd, packed_ref, best_ref, asg_ref, sums_ref, wts_ref):
    low = (kd + 1) * cd
    best_ref[...] = packed_ref[low : low + 1, 0:pd]
    asg_ref[...] = packed_ref[low + 1 : low + 2, 0:pd]
    for k in range(kd):
        sums_ref[:, k, :] = packed_ref[k * cd : (k + 1) * cd, :]
    weights = packed_ref[kd * cd : (kd + 1) * cd, :].T
    wts_ref[...] = weights[0:kd, :] + weights[kd : 2 * kd, :]


def on_device(dims, images, references, ctf, class_ids, rot_ids, group_ids):
    ny, nx, nz, pd, cy, modes, cd = dims
    ndp, width, ncls = ny * nx, 2 * modes, nz * CORES * cd
    kd = cy // ndp
    hops = nz // 2
    block = kd * pd + 16
    most = 3 * cd
    row = lambda ids: ids.reshape(1, pd)
    vmem = pl.BlockSpec(memory_space=pltpu.VMEM)
    dma = pltpu.SemaphoreType.DMA
    packed = pl.pallas_call(
        functools.partial(kernel, dims),
        out_shape=jax.ShapeDtypeStruct(((kd + 1) * cd + 8, width), F32),
        in_specs=[vmem] * 7,
        out_specs=vmem,
        scratch_shapes=[
            pltpu.VMEM((pd, cy, width), BF16),
            pltpu.VMEM((8, 2 * pd), I32),
            pltpu.VMEM((8, 2 * pd), I32),
            pltpu.VMEM((2 * pd * (cy + 1), width), F32),
            pltpu.VMEM((cy * (width + 1), 2 * pd), F32),
            pltpu.VMEM((modes, 2 * cy, 4 * pd), BF16),
            pltpu.VMEM((cd * (modes + 1), 2 * cy), F32),
            pltpu.VMEM((nz, modes, cd, 2 * cy), BF16),
            pltpu.VMEM((modes, most, 4 * pd), F32),
            pltpu.VMEM((cy, 2 * pd), F32),
            pltpu.VMEM((16, 2 * pd), F32),
            pltpu.VMEM((ndp, block, width), BF16),
            pltpu.VMEM((ndp, block, width), BF16),
            pltpu.VMEM((ncls, ndp * pd), BF16),
            pltpu.VMEM((16, ndp * pd), BF16),
            pltpu.VMEM((kd, ncls, width), F32),
            pltpu.VMEM((ncls, width), F32),
            pltpu.VMEM((kd, nz, 2 * cd, width), BF16),
            pltpu.VMEM((kd, nz, 2 * cd, width), BF16),
            pltpu.VMEM((kd, nz, 2 * cd, width), BF16),
            pltpu.VMEM((kd, nz, 2 * cd, width), BF16),
            pltpu.VMEM((8, 2 * pd), F32),
            pltpu.VMEM((8, 2 * pd), F32),
            pltpu.VMEM((8, 2 * pd), F32),
            pltpu.VMEM((8, 2 * pd), F32),
            dma((2, hops, 2)),
            dma((2, hops, 2)),
            dma((kd, ndp)),
            dma((kd, ndp)),
            dma((kd,)),
            dma((kd,)),
            dma((kd, nz)),
            dma((kd, nz)),
            dma((3,)),
            dma((3,)),
        ],
        compiler_params=pltpu.CompilerParams(
            collective_id=0, has_side_effects=True, vmem_limit_bytes=60 * 1024 * 1024
        ),
    )(
        jnp.asarray(turn_table(modes)), images, references, ctf.T, row(class_ids), row(rot_ids), row(group_ids)
    )
    best, assigned, sums, weights = pl.pallas_call(
        functools.partial(deliver, pd, cd, kd),
        out_shape=(
            jax.ShapeDtypeStruct((1, pd), F32),
            jax.ShapeDtypeStruct((1, pd), F32),
            jax.ShapeDtypeStruct((cd, kd, width), F32),
            jax.ShapeDtypeStruct((kd, cd), F32),
        ),
        in_specs=[vmem],
        out_specs=(vmem,) * 4,
    )(packed)
    return best.reshape(pd), assigned.reshape(pd), sums, weights.T


def plane(count):
    side = 1
    while side * side < count:
        side *= 2
    return count // side, side


def solution(mesh):
    ndp, ncl = mesh.shape["dp"], mesh.shape["cls"]
    ny, nx = plane(ndp)

    def step(images, references, ctf, class_ids, rot_ids, group_ids):
        pd, cy, width = images.shape
        dims = (ny, nx, ncl // CORES, pd, cy, width // 2, references.shape[0])
        return on_device(dims, images, references, ctf, class_ids, rot_ids, group_ids)

    both = P(("dp", "cls"))
    return jax.shard_map(
        step,
        mesh=mesh,
        in_specs=(P(("dp", "cls"), None, None), P("cls", None, None), P(), P(("dp", "cls"), None), both, both),
        out_specs=(both, both, P("cls", "dp", None), P("cls", "dp")),
        check_vma=False,
    )
```

```python
import functools
import math

import jax
import jax.numpy as jnp
import numpy as np
from jax import lax
from jax.experimental import pallas as pl
from jax.experimental.pallas import tpu as pltpu
from jax.sharding import PartitionSpec as P

ROT = 36
HALF = ROT // 2
QUART = ROT // 4
CORES = 2
F32 = jnp.float32
BF16 = jnp.bfloat16
I32 = jnp.int32
MESH = pl.DeviceIdType.MESH
HIGHEST = lax.Precision.HIGHEST


def bf16_value(x):
    return float(np.float32(x).astype(BF16))


def turn_table(modes):
    order = (np.arange(ROT)[:, None] * np.arange(modes)[None, :]) % ROT
    angle = order * (2.0 * math.pi / ROT)
    cos, sin = np.cos(angle), np.sin(angle)
    table = np.zeros((64, 4 * modes), np.float32)
    table[:ROT] = np.concatenate([cos, cos, -sin, sin], axis=1)
    return table


def weighted_sum(terms):
    groups = {}
    for coefficient, value in terms:
        size = round(abs(coefficient), 12)
        if size < 1e-9:
            continue
        groups.setdefault(size, []).append((coefficient > 0, value))
    total = None
    for size, members in groups.items():
        part = None
        for positive, value in members:
            if part is None:
                part = value if positive else -value
            else:
                part = part + value if positive else part - value
        if size != 1.0:
            part = part * F32(bf16_value(size))
        total = part if total is None else total + part
    return total


def rotation_scores(re, im, modes):
    fold_re, fold_im = [None] * ROT, [None] * ROT
    for m in range(modes):
        for fold, part in ((fold_re, re), (fold_im, im)):
            at = m % ROT
            fold[at] = part(m) if fold[at] is None else fold[at] + part(m)
    even = [None] * (HALF + 1)
    odd = [None] * (HALF + 1)
    even[0], even[HALF] = fold_re[0], fold_re[HALF]
    for m in range(1, HALF):
        even[m] = fold_re[m] + fold_re[ROT - m]
        odd[m] = fold_im[m] - fold_im[ROT - m]
    scores = {}
    for r in range(QUART + 1):
        cos = lambda m: math.cos(2.0 * math.pi * ((m * r) % ROT) / ROT)
        sin = lambda m: math.sin(2.0 * math.pi * ((m * r) % ROT) / ROT)
        ce = weighted_sum([(cos(m), even[m]) for m in range(0, HALF + 1, 2)])
        co = weighted_sum([(cos(m), even[m]) for m in range(1, HALF + 1, 2)])
        se = weighted_sum([(sin(m), odd[m]) for m in range(2, HALF, 2)])
        so = weighted_sum([(sin(m), odd[m]) for m in range(1, HALF, 2)])
        if r == 0:
            scores[0], scores[HALF] = ce + co, ce - co
        elif r == QUART:
            scores[r], scores[ROT - r] = ce - so, ce + so
        else:
            plus, minus, both, apart = ce + co, ce - co, se + so, se - so
            scores[r], scores[ROT - r] = plus - both, plus + both
            scores[HALF - r], scores[HALF + r] = minus + apart, minus - apart
    return scores


def kernel(
    dims,
    tab_hbm, img_hbm, refs_hbm, ctft_hbm, cid_hbm, rid_hbm, gid_hbm,
    out_ref,
    tab_ref, img_ref, refs_ref, ctft_ref, cid_ref, rid_ref, gid_ref,
    img_rx, ids_tx, ids_rx, xs, s2, rhs, s3, slots, xm, cts, tail, a_tx, a_rx,
    hot, wrow, facc, wacc, p_tx, p_rx, r_tx, r_rx, best_acc, asg_acc, e_tx, e_rx,
    ag_s, ag_r, aa_s, aa_r, pt_s, pt_r, rs_s, rs_r, one_s, one_r, in_s,
):
    ny, nx, nz, pd, cy, modes, cd = dims
    ndp, width, ncls = ny * nx, 2 * modes, nz * CORES * cd
    kd = cy // ndp
    hops, half = nz // 2, modes // 2
    px, pk, pm = cy + 1, width + 1, modes + 1
    dp, cls = lax.axis_index("dp"), lax.axis_index("cls")
    z, core = cls // CORES, cls % CORES
    y, x = dp // nx, dp % nx
    partner = (dp, z * CORES + 1 - core)

    def z_peer(step):
        return (dp, ((z + step + nz) % nz) * CORES + core)

    def dp_peer(step):
        return ((y + step // nx) % ny) * nx + (x + step % nx) % nx

    def remote(src, dst, send, recv, device):
        return pltpu.make_async_remote_copy(
            src_ref=src, dst_ref=dst, send_sem=send, recv_sem=recv, device_id=device, device_id_type=MESH
        )

    fetches = []
    for at, (source, target) in enumerate((
        (refs_hbm, refs_ref), (cid_hbm, cid_ref), (rid_hbm, rid_ref), (gid_hbm, gid_ref),
        (ctft_hbm, ctft_ref), (tab_hbm, tab_ref), (img_hbm, img_ref),
    )):
        fetches.append(pltpu.make_async_copy(source, target, in_s.at[at]))
        fetches[-1].start()

    barrier = pltpu.get_barrier_semaphore()
    pl.semaphore_signal(barrier, inc=1, device_id=partner, device_id_type=MESH)
    for step in range(1, nz):
        pl.semaphore_signal(barrier, inc=1, device_id=z_peer(step), device_id_type=MESH)

    def greet(step, carry):
        pl.semaphore_signal(barrier, inc=1, device_id=(dp_peer(step), cls), device_id_type=MESH)
        return carry

    lax.fori_loop(1, ndp, greet, 0)

    for fetch in fetches[1:4]:
        fetch.wait()
    ids_tx[...] = jnp.zeros_like(ids_tx)
    ids_tx[0:1, 0:pd] = cid_ref[...]
    ids_tx[1:2, 0:pd] = rid_ref[...]
    ids_tx[2:3, 0:pd] = gid_ref[...]
    img_copy = remote(img_hbm, img_rx, one_s.at[0], one_r.at[0], partner)
    ids_copy = remote(ids_tx, ids_rx, one_s.at[1], one_r.at[1], partner)

    lane_k = lax.broadcasted_iota(I32, (modes, 2 * cy), 1)

    def ref_pair(p, carry):
        both = refs_ref[pl.ds(2 * p, 2)].astype(F32).reshape(2 * cy, width)
        turned = both.T
        re, im = turned[:modes], turned[modes:]
        s3[pl.ds(2 * p * pm, modes), :] = jnp.where(lane_k < cy, re, pltpu.roll(im, cy, 1))
        s3[pl.ds((2 * p + 1) * pm, modes), :] = jnp.where(
            lane_k < cy, pltpu.roll(re, cy, 1), im
        )
        return carry

    fetches[0].wait()
    lax.fori_loop(0, cd // 2, ref_pair, 0, unroll=4)

    def ag(way, hop, part):
        src = 0 if hop == 0 else 2 * hop - 1 + way
        dst = nz - 1 if hop == hops - 1 else 2 * hop + 1 + way
        span = pl.ds(part * half, half)
        return remote(
            slots.at[src, span], slots.at[dst, span], ag_s.at[0], ag_r.at[2 * (2 * hop + part) + way],
            z_peer(1 - 2 * way),
        )

    def ag_sent(way, hop, part):
        return hop < hops - 1 or part == way

    def ref_mode(m, carry):
        slots[0, m] = s3[pl.ds(m, cd, stride=pm), :].astype(BF16)
        return carry

    lax.fori_loop(0, modes, ref_mode, 0, unroll=8)

    def fill(base, image, groups):
        hot_g = (lax.broadcasted_iota(I32, (ctft_ref.shape[1], 2 * pd), 0) == groups).astype(F32)
        weights = jnp.dot(ctft_ref[...], hot_g, precision=HIGHEST, preferred_element_type=F32)

        def body(block, carry):
            for u in range(8):
                at = block * 8 + u
                xs[pl.ds((base + at) * px, cy), :] = image[at].astype(F32) * carry[:, u : u + 1]
            return pltpu.roll(carry, 2 * pd - 8, 1)

        lax.fori_loop(0, pd // 8, body, weights)
        return weights

    for fetch in fetches[4:]:
        fetch.wait()
    cts[...] = fill(0, img_ref, ids_tx[2:3, :])

    pl.semaphore_wait(barrier, nz + ndp - 1)
    for part in range(2):
        for way in range(2):
            if ag_sent(way, 0, part):
                ag(way, 0, part).start()
    ids_copy.start()
    img_copy.start()

    eye = lax.broadcasted_iota(I32, (pd, 2 * pd), 0) == lax.broadcasted_iota(I32, (pd, 2 * pd), 1)
    rot_col = jnp.sum(jnp.where(eye, ids_tx[1:2, :].astype(F32), 0.0), axis=1, keepdims=True)
    rot_hot = (lax.broadcasted_iota(I32, (pd, 64), 1).astype(F32) == rot_col).astype(F32)
    table = jnp.dot(rot_hot, tab_ref[...], precision=HIGHEST, preferred_element_type=F32)
    cosine, sine = table[:, :width], table[:, width:]
    tail[...] = jnp.zeros_like(tail)
    lane_p = lax.broadcasted_iota(I32, (1, 2 * pd), 1)
    tail[2 * kd : 2 * kd + 1, :] = jnp.where(lane_p < pd, ids_tx[0:1, :].astype(F32), 0.0)

    def turn_to(k, step, target):
        cycle = dp_peer(step) * kd + k
        row = xs[pl.ds(cycle, pd, stride=px), :]
        spun = row * cosine + pltpu.roll(row, modes, 1) * sine
        target[step, 16 + k * pd : 16 + (k + 1) * pd, :] = spun.astype(BF16)
        if k == 0:
            for at in range(kd):
                weight = cts[pl.ds(cycle + at, 1), :]
                square = jnp.where(lane_p < pd, weight * weight, 0.0)
                high = square.astype(BF16).astype(F32)
                tail[at : at + 1, :] = high
                tail[kd + at : kd + at + 1, :] = square - high
            target[step, 0:16, :] = tail[...].astype(BF16)

    def a2a(k, step):
        span = pl.ds(0, 16 + pd) if k == 0 else pl.ds(16 + k * pd, pd)
        return remote(
            a_tx.at[step, span], a_rx.at[step, span], aa_s.at[0], aa_r.at[k], (dp_peer(step), cls)
        )

    def a2a_all(k):
        span = pl.ds(0, 16 + pd) if k == 0 else pl.ds(16 + k * pd, pd)
        peers = pl.ds(1, ndp - 1)
        return remote(a_tx.at[peers, span], a_rx.at[peers, span], aa_s.at[0], aa_r.at[k], (dp_peer(1), cls))

    for k in range(kd):

        def send_turned(step, carry):
            turn_to(k, step, a_tx)
            a2a(k, step).start()
            return carry

        lax.fori_loop(1, ndp, send_turned, 0, unroll=5)
        turn_to(k, 0, a_rx)

    def forward(hop, part):
        for way in range(2):
            if ag_sent(way, hop, part):
                ag(way, hop - 1, part).wait_recv()
                ag(way, hop, part).start()
            elif hop < hops - 1:
                ag(way, hop - 1, part).wait_recv()

    ids_copy.wait_recv()
    img_copy.wait_recv()
    fill(pd, img_rx, ids_rx[2:3, :])
    forward(1, 0)

    def flip(k, carry):
        s2[pl.ds(k * pk, width), :] = xs[pl.ds(k, 2 * pd, stride=px), :].T
        return carry

    lax.fori_loop(0, cy, flip, 0, unroll=4)

    def spread(m, carry):
        re = s2[pl.ds(m, cy, stride=pk), :]
        im = s2[pl.ds(m + modes, cy, stride=pk), :]
        rhs[m, 0:cy, 0 : 2 * pd] = re.astype(BF16)
        rhs[m, 0:cy, 2 * pd : 4 * pd] = (-im).astype(BF16)
        rhs[m, cy : 2 * cy, 0 : 2 * pd] = im.astype(BF16)
        rhs[m, cy : 2 * cy, 2 * pd : 4 * pd] = re.astype(BF16)
        return carry

    lax.fori_loop(0, modes, spread, 0, unroll=4)
    forward(1, 1)

    lane2 = lax.broadcasted_iota(I32, (8, 2 * pd), 1)
    ids_all = jnp.where(lane2 < pd, ids_tx[...], pltpu.roll(ids_rx[...], pd, 1))
    class_row, rot_row = ids_all[0:1, :], ids_all[1:2, :]
    best_acc[...] = jnp.full_like(best_acc, -1e30)
    asg_acc[...] = jnp.zeros_like(asg_acc)
    sub8 = lax.broadcasted_iota(I32, (8, 2 * pd), 0)

    def score(first, count, between=None):
        high = count * cd

        def cross(m, carry):
            left = slots[first : first + count, m].reshape(high, 2 * cy)
            xm[m, 0:high, :] = jnp.dot(left, rhs[m], preferred_element_type=F32)
            return carry

        lax.fori_loop(0, modes, cross, 0, unroll=32)

        def column(col, carry):
            at = pl.multiple_of(col * 8, 8)
            slot = first + at // cd
            hop = (slot + 1) // 2
            source = (z + jnp.where(slot % 2 == 1, -hop, hop) + nz) % nz
            base = (source * CORES + core) * cd + at % cd
            re = lambda m: xm[m, pl.ds(at, 8), 0 : 2 * pd]
            im = lambda m: xm[m, pl.ds(at, 8), 2 * pd : 4 * pd]
            scores = rotation_scores(re, im, modes)
            top, chosen = None, jnp.zeros((8, 2 * pd), F32)
            for r, value in scores.items():
                top = value if top is None else jnp.maximum(top, value)
                chosen = jnp.where(rot_row == r, value, chosen)
            best_acc[...] = jnp.maximum(best_acc[...], top)
            asg_acc[...] = asg_acc[...] + jnp.where(class_row == base + sub8, chosen, 0.0)
            return carry

        lax.fori_loop(0, high // 8, column, 0)

    def one_hot():
        class_iota = lax.broadcasted_iota(I32, (ncls, 2 * pd), 0).astype(F32)
        for q in range(ndp // 2):
            near = a_rx[2 * q, 0:16, :].astype(F32)
            both = near + pltpu.roll(a_rx[2 * q + 1, 0:16, :].astype(F32), pd, 1)
            at = slice(q * 2 * pd, (q + 1) * 2 * pd)
            hot[:, at] = (class_iota == both[2 * kd : 2 * kd + 1, :]).astype(F32).astype(BF16)
            wrow[:, at] = both.astype(BF16)
        wacc[...] = jnp.zeros_like(wacc)
        wacc[:, 0:16] = lax.dot_general(hot[...], wrow[...], (((1,), (1,)), ((), ())), preferred_element_type=F32)

    def tiles(k):
        return 2 * cd if k == 0 else cd

    def at_class(owner):
        return pl.ds(pl.multiple_of(owner * cd, cd), cd)

    def with_rest(weights):
        high = weights.astype(BF16).astype(F32)
        return (high + pltpu.roll(weights - high, 16, 1)).astype(BF16)

    def without_rest(block):
        return block + pltpu.roll(block, width - 16, 1)

    def to_partner(k):
        span = pl.ds(0, tiles(k))
        return remote(p_tx.at[k, :, span], p_rx.at[k, :, span], pt_s.at[k], pt_r.at[k], partner)

    def to_owner(k, step):
        span = pl.ds(0, tiles(k))
        return remote(
            r_tx.at[k, step, span], r_rx.at[k, step, span], rs_s.at[k], rs_r.at[k], z_peer(step)
        )

    def to_owner_all(k):
        span, peers = pl.ds(0, tiles(k)), pl.ds(1, nz - 1)
        return remote(r_tx.at[k, peers, span], r_rx.at[k, peers, span], rs_s.at[k], rs_r.at[k], z_peer(1))

    def sum_cycle(k):
        a2a_all(k).wait_recv()
        if k == 0:
            one_hot()
        right = a_rx[:, 16 + k * pd : 16 + (k + 1) * pd, :].reshape(ndp * pd, width)
        facc[k] = jnp.dot(hot[...], right, preferred_element_type=F32)

        for chip in range(nz):
            at = at_class(chip * CORES + 1 - core)
            p_tx[k, chip, 0:cd, :] = facc[k, at, :].astype(BF16)
            if k == 0:
                p_tx[k, chip, cd : 2 * cd, :] = with_rest(wacc[at, :])
        to_partner(k).start()

    def chip_cycle(k):
        to_partner(k).wait_recv()

        def chip_sum(step):
            chip = (z + step) % nz
            at = at_class(chip * CORES + core)
            values = facc[k, at, :] + p_rx[k, chip, 0:cd, :].astype(F32)
            return values, (wacc[at, :] + without_rest(p_rx[k, chip, cd : 2 * cd, :].astype(F32)) if k == 0 else None)

        keep = lax.broadcasted_iota(I32, (cd, width), 1) < 16
        for step in range(1, nz):
            values, weights = chip_sum(step)
            r_tx[k, step, 0:cd, :] = values.astype(BF16)
            if k == 0:
                r_tx[k, step, cd : 2 * cd, :] = with_rest(jnp.where(keep, weights, 0.0))
        for step in sorted(range(1, nz), key=lambda step: -min(step, nz - step)):
            to_owner(k, step).start()
        values, weights = chip_sum(0)
        out_ref[k * cd : (k + 1) * cd, :] = values
        if k == 0:
            out_ref[kd * cd : (kd + 1) * cd, :] = weights

    def owned_cycle(k):
        to_owner_all(k).wait_recv()
        at = slice(k * cd, (k + 1) * cd)
        out_ref[at, :] = out_ref[at, :] + sum(r_rx[k, step, 0:cd, :].astype(F32) for step in range(1, nz))
        if k == 0:
            at = slice(kd * cd, (kd + 1) * cd)
            rest = sum(r_rx[k, step, cd : 2 * cd, :].astype(F32) for step in range(1, nz))
            out_ref[at, :] = out_ref[at, :] + without_rest(rest)

    todo = []
    for k in range(kd):
        todo.append((sum_cycle, k))
        if k > 0:
            todo.append((chip_cycle, k - 1))
    todo.append((chip_cycle, kd - 1))

    def some(count):
        for _ in range(min(count, len(todo))):
            act, k = todo.pop(0)
            act(k)

    some(1)
    done = 0
    for hop in range(2, hops):
        score(done, 2 * hop - 1 - done)
        done = 2 * hop - 1
        forward(hop, 0)
        some(2)
        forward(hop, 1)

    some(len(todo))

    for part in range(2):
        for way in range(2):
            if not ag_sent(way, hops - 1, part):
                ag(way, hops - 2, part).wait_recv()
    score(done, nz - 1 - done)
    for way in range(2):
        ag(way, hops - 1, way).wait_recv()
    score(nz - 1, 1)

    e_tx[...] = jnp.zeros_like(e_tx)
    e_tx[0:1, :] = jnp.max(best_acc[...], axis=0, keepdims=True)
    e_tx[1:2, :] = jnp.sum(asg_acc[...], axis=0, keepdims=True)
    e_copy = remote(e_tx, e_rx, one_s.at[2], one_r.at[2], partner)
    e_copy.start()

    for k in range(kd):
        owned_cycle(k)

    e_copy.wait_recv()
    other = pltpu.roll(e_rx[...], pd, 1)
    low = (kd + 1) * cd
    out_ref[low : low + 1, :] = jnp.maximum(e_tx[0:1, :], other[0:1, :])
    out_ref[low + 1 : low + 2, :] = e_tx[1:2, :] + other[1:2, :]
    out_ref[low + 2 : low + 8, :] = jnp.zeros((6, width), F32)

    gone = slots.at[pl.ds(0, nz - 1)]
    remote(gone, gone, ag_s.at[0], ag_r.at[0], z_peer(1)).wait_send()
    gone = pl.ds(1, ndp - 1)
    remote(a_tx.at[gone], a_rx.at[gone], aa_s.at[0], aa_r.at[0], (dp_peer(1), cls)).wait_send()
    for k in range(kd):
        to_owner_all(k).wait_send()
        to_partner(k).wait_send()
    for copy in (img_copy, ids_copy, e_copy):
        copy.wait_send()


def deliver(pd, cd, kd, packed_ref, best_ref, asg_ref, sums_ref, wts_ref):
    low = (kd + 1) * cd
    best_ref[...] = packed_ref[low : low + 1, 0:pd]
    asg_ref[...] = packed_ref[low + 1 : low + 2, 0:pd]
    for k in range(kd):
        sums_ref[:, k, :] = packed_ref[k * cd : (k + 1) * cd, :]
    weights = packed_ref[kd * cd : (kd + 1) * cd, :].T
    wts_ref[...] = weights[0:kd, :] + weights[kd : 2 * kd, :]


def on_device(dims, images, references, ctf, class_ids, rot_ids, group_ids):
    ny, nx, nz, pd, cy, modes, cd = dims
    ndp, width, ncls = ny * nx, 2 * modes, nz * CORES * cd
    kd = cy // ndp
    hops = nz // 2
    block = kd * pd + 16
    most = 3 * cd
    row = lambda ids: ids.reshape(1, pd)
    vmem = pl.BlockSpec(memory_space=pltpu.VMEM)
    dma = pltpu.SemaphoreType.DMA
    packed = pl.pallas_call(
        functools.partial(kernel, dims),
        out_shape=jax.ShapeDtypeStruct(((kd + 1) * cd + 8, width), F32),
        in_specs=[pl.BlockSpec(memory_space=pl.ANY)] * 7,
        out_specs=vmem,
        scratch_shapes=[
            pltpu.VMEM((64, 2 * width), F32),
            pltpu.VMEM((pd, cy, width), BF16),
            pltpu.VMEM((cd, cy, width), BF16),
            pltpu.VMEM((cy, ctf.shape[0]), F32),
            pltpu.VMEM((1, pd), I32),
            pltpu.VMEM((1, pd), I32),
            pltpu.VMEM((1, pd), I32),
            pltpu.VMEM((pd, cy, width), BF16),
            pltpu.VMEM((8, 2 * pd), I32),
            pltpu.VMEM((8, 2 * pd), I32),
            pltpu.VMEM((2 * pd * (cy + 1), width), F32),
            pltpu.VMEM((cy * (width + 1), 2 * pd), F32),
            pltpu.VMEM((modes, 2 * cy, 4 * pd), BF16),
            pltpu.VMEM((cd * (modes + 1), 2 * cy), F32),
            pltpu.VMEM((nz, modes, cd, 2 * cy), BF16),
            pltpu.VMEM((modes, most, 4 * pd), F32),
            pltpu.VMEM((cy, 2 * pd), F32),
            pltpu.VMEM((16, 2 * pd), F32),
            pltpu.VMEM((ndp, block, width), BF16),
            pltpu.VMEM((ndp, block, width), BF16),
            pltpu.VMEM((ncls, ndp * pd), BF16),
            pltpu.VMEM((16, ndp * pd), BF16),
            pltpu.VMEM((kd, ncls, width), F32),
            pltpu.VMEM((ncls, width), F32),
            pltpu.VMEM((kd, nz, 2 * cd, width), BF16),
            pltpu.VMEM((kd, nz, 2 * cd, width), BF16),
            pltpu.VMEM((kd, nz, 2 * cd, width), BF16),
            pltpu.VMEM((kd, nz, 2 * cd, width), BF16),
            pltpu.VMEM((8, 2 * pd), F32),
            pltpu.VMEM((8, 2 * pd), F32),
            pltpu.VMEM((8, 2 * pd), F32),
            pltpu.VMEM((8, 2 * pd), F32),
            dma((1,)),
            dma((4 * hops,)),
            dma((1,)),
            dma((kd,)),
            dma((kd,)),
            dma((kd,)),
            dma((kd,)),
            dma((kd,)),
            dma((3,)),
            dma((3,)),
            dma((7,)),
        ],
        compiler_params=pltpu.CompilerParams(
            collective_id=0, has_side_effects=True, vmem_limit_bytes=60 * 1024 * 1024
        ),
    )(
        jnp.asarray(turn_table(modes)), images, references, ctf.T, row(class_ids), row(rot_ids), row(group_ids)
    )
    best, assigned, sums, weights = pl.pallas_call(
        functools.partial(deliver, pd, cd, kd),
        out_shape=(
            jax.ShapeDtypeStruct((1, pd), F32),
            jax.ShapeDtypeStruct((1, pd), F32),
            jax.ShapeDtypeStruct((cd, kd, width), F32),
            jax.ShapeDtypeStruct((kd, cd), F32),
        ),
        in_specs=[vmem],
        out_specs=(vmem,) * 4,
    )(packed)
    return best.reshape(pd), assigned.reshape(pd), sums, weights.T


def plane(count):
    side = 1
    while side * side < count:
        side *= 2
    return count // side, side


def solution(mesh):
    ndp, ncl = mesh.shape["dp"], mesh.shape["cls"]
    ny, nx = plane(ndp)

    def step(images, references, ctf, class_ids, rot_ids, group_ids):
        pd, cy, width = images.shape
        dims = (ny, nx, ncl // CORES, pd, cy, width // 2, references.shape[0])
        return on_device(dims, images, references, ctf, class_ids, rot_ids, group_ids)

    both = P(("dp", "cls"))
    return jax.shard_map(
        step,
        mesh=mesh,
        in_specs=(P(("dp", "cls"), None, None), P("cls", None, None), P(), P(("dp", "cls"), None), both, both),
        out_specs=(both, both, P("cls", "dp", None), P("cls", "dp")),
        check_vma=False,
    )
```

```python
import functools
import math

import jax
import jax.numpy as jnp
import numpy as np
from jax import lax
from jax.experimental import pallas as pl
from jax.experimental.pallas import tpu as pltpu
from jax.sharding import PartitionSpec as P

ROT = 36
HALF = ROT // 2
QUART = ROT // 4
CORES = 2
F32 = jnp.float32
BF16 = jnp.bfloat16
I32 = jnp.int32
MESH = pl.DeviceIdType.MESH
HIGHEST = lax.Precision.HIGHEST


def bf16_value(x):
    return float(np.float32(x).astype(BF16))


def turn_table(modes):
    order = (np.arange(ROT)[:, None] * np.arange(modes)[None, :]) % ROT
    angle = order * (2.0 * math.pi / ROT)
    cos, sin = np.cos(angle), np.sin(angle)
    table = np.zeros((64, 4 * modes), np.float32)
    table[:ROT] = np.concatenate([cos, cos, -sin, sin], axis=1)
    return table


def weighted_sum(terms):
    groups = {}
    for coefficient, value in terms:
        size = round(abs(coefficient), 12)
        if size < 1e-9:
            continue
        groups.setdefault(size, []).append((coefficient > 0, value))
    total = None
    for size, members in groups.items():
        part = None
        for positive, value in members:
            if part is None:
                part = value if positive else -value
            else:
                part = part + value if positive else part - value
        if size != 1.0:
            part = part * F32(bf16_value(size))
        total = part if total is None else total + part
    return total


def rotation_scores(re, im, modes):
    fold_re, fold_im = [None] * ROT, [None] * ROT
    for m in range(modes):
        for fold, part in ((fold_re, re), (fold_im, im)):
            at = m % ROT
            fold[at] = part(m) if fold[at] is None else fold[at] + part(m)
    even = [None] * (HALF + 1)
    odd = [None] * (HALF + 1)
    even[0], even[HALF] = fold_re[0], fold_re[HALF]
    for m in range(1, HALF):
        even[m] = fold_re[m] + fold_re[ROT - m]
        odd[m] = fold_im[m] - fold_im[ROT - m]
    scores = {}
    for r in range(QUART + 1):
        cos = lambda m: math.cos(2.0 * math.pi * ((m * r) % ROT) / ROT)
        sin = lambda m: math.sin(2.0 * math.pi * ((m * r) % ROT) / ROT)
        ce = weighted_sum([(cos(m), even[m]) for m in range(0, HALF + 1, 2)])
        co = weighted_sum([(cos(m), even[m]) for m in range(1, HALF + 1, 2)])
        se = weighted_sum([(sin(m), odd[m]) for m in range(2, HALF, 2)])
        so = weighted_sum([(sin(m), odd[m]) for m in range(1, HALF, 2)])
        if r == 0:
            scores[0], scores[HALF] = ce + co, ce - co
        elif r == QUART:
            scores[r], scores[ROT - r] = ce - so, ce + so
        else:
            plus, minus, both, apart = ce + co, ce - co, se + so, se - so
            scores[r], scores[ROT - r] = plus - both, plus + both
            scores[HALF - r], scores[HALF + r] = minus + apart, minus - apart
    return scores


def kernel(
    dims,
    tab_hbm, img_hbm, refs_hbm, ctft_hbm, cid_hbm, rid_hbm, gid_hbm,
    out_ref,
    tab_ref, img_ref, refs_ref, ctft_ref, cid_ref, rid_ref, gid_ref,
    img_rx, ids_tx, ids_rx, xs, s2, rhs, s3, slots, xm, cts, tail, a_tx, a_rx,
    hot, wrow, facc, wacc, p_tx, p_rx, r_tx, r_rx, best_acc, asg_acc, e_tx, e_rx,
    ag_s, ag_r, sd_r, aa_s, aa_r, pt_s, pt_r, rs_s, rs_r, one_s, one_r, in_s,
):
    ny, nx, nz, pd, cy, modes, cd = dims
    ndp, width, ncls = ny * nx, 2 * modes, nz * CORES * cd
    kd = cy // ndp
    hops, half = nz // 2, modes // 2
    px, pk, pm = cy + 1, width + 1, modes + 1
    dp, cls = lax.axis_index("dp"), lax.axis_index("cls")
    z, core = cls // CORES, cls % CORES
    y, x = dp // nx, dp % nx
    partner = (dp, z * CORES + 1 - core)

    def z_peer(step):
        return (dp, ((z + step + nz) % nz) * CORES + core)

    def dp_peer(step):
        return ((y + step // nx) % ny) * nx + (x + step % nx) % nx

    def remote(src, dst, send, recv, device):
        return pltpu.make_async_remote_copy(
            src_ref=src, dst_ref=dst, send_sem=send, recv_sem=recv, device_id=device, device_id_type=MESH
        )

    fetches = []
    for at, (source, target) in enumerate((
        (refs_hbm, refs_ref), (cid_hbm, cid_ref), (rid_hbm, rid_ref), (gid_hbm, gid_ref),
        (ctft_hbm, ctft_ref), (tab_hbm, tab_ref), (img_hbm, img_ref),
    )):
        fetches.append(pltpu.make_async_copy(source, target, in_s.at[at]))
        fetches[-1].start()

    barrier = pltpu.get_barrier_semaphore()
    pl.semaphore_signal(barrier, inc=1, device_id=partner, device_id_type=MESH)
    for step in range(1, nz):
        pl.semaphore_signal(barrier, inc=1, device_id=z_peer(step), device_id_type=MESH)

    def greet(step, carry):
        pl.semaphore_signal(barrier, inc=1, device_id=(dp_peer(step), cls), device_id_type=MESH)
        return carry

    lax.fori_loop(1, ndp, greet, 0)

    for fetch in fetches[1:4]:
        fetch.wait()
    ids_tx[...] = jnp.zeros_like(ids_tx)
    ids_tx[0:1, 0:pd] = cid_ref[...]
    ids_tx[1:2, 0:pd] = rid_ref[...]
    ids_tx[2:3, 0:pd] = gid_ref[...]
    img_copy = remote(img_hbm, img_rx, one_s.at[0], one_r.at[0], partner)
    ids_copy = remote(ids_tx, ids_rx, one_s.at[1], one_r.at[1], partner)

    lane_k = lax.broadcasted_iota(I32, (modes, 2 * cy), 1)

    def ref_pair(p, carry):
        both = refs_ref[pl.ds(2 * p, 2)].astype(F32).reshape(2 * cy, width)
        turned = both.T
        re, im = turned[:modes], turned[modes:]
        s3[pl.ds(2 * p * pm, modes), :] = jnp.where(lane_k < cy, re, pltpu.roll(im, cy, 1))
        s3[pl.ds((2 * p + 1) * pm, modes), :] = jnp.where(
            lane_k < cy, pltpu.roll(re, cy, 1), im
        )
        return carry

    fetches[0].wait()
    lax.fori_loop(0, cd // 2, ref_pair, 0, unroll=4)

    color = (x + y) % 2
    quarter = modes // 4

    def slot_of(way, hop):
        return 0 if hop == 0 else nz - 1 if hop == hops else 2 * hop - 1 + way

    def piece_at(piece):
        return pl.ds(pl.multiple_of((color + piece // 2) % 2 * half + piece % 2 * quarter, quarter), quarter)

    def ag(way, hop, piece):
        at = 2 * piece + way if hop == 0 else 4 * (hop + 1) + 2 * piece + way
        return remote(
            slots.at[slot_of(way, hop), piece_at(piece)], slots.at[slot_of(way, hop + 1), piece_at(piece)],
            ag_s.at[0], ag_r.at[at], z_peer(1 - 2 * way),
        )

    def start_both(piece):
        for way in range(2):
            ag(way, 0, piece).start()

    def side(slot, axis):
        to = ((y + (ny - 1) * axis) % ny) * nx + (x + (nx - 1) * (1 - axis)) % nx
        ref = slots.at[slot, piece_at(axis)]
        return remote(ref, ref, ag_s.at[1], sd_r.at[slot], (to, cls))

    def complete(*wanted):
        for slot in wanted:
            ref = slots.at[slot, pl.ds(pl.multiple_of((color + 1) % 2 * half, half), half)]
            remote(ref, ref, ag_s.at[1], sd_r.at[slot], partner).wait_recv()

    def forward(hop, piece):
        for way in range(2):
            ag(way, hop - 1, piece).wait_recv()
            if hop < hops - 1 or piece == way:
                ag(way, hop, piece).start()
            if hop > 1:
                side(slot_of(way, hop), piece).start()

    def forward_far(way):
        ag(way, hops - 1, way).wait_recv()
        side(nz - 1, way).start()

    def ref_mode(m, carry):
        slots[0, m] = s3[pl.ds(m, cd, stride=pm), :].astype(BF16)
        return carry

    lax.fori_loop(0, modes, ref_mode, 0, unroll=8)

    def fill(base, image, groups):
        hot_g = (lax.broadcasted_iota(I32, (ctft_ref.shape[1], 2 * pd), 0) == groups).astype(F32)
        weights = jnp.dot(ctft_ref[...], hot_g, precision=HIGHEST, preferred_element_type=F32)

        def body(block, carry):
            for u in range(8):
                at = block * 8 + u
                xs[pl.ds((base + at) * px, cy), :] = image[at].astype(F32) * carry[:, u : u + 1]
            return pltpu.roll(carry, 2 * pd - 8, 1)

        lax.fori_loop(0, pd // 8, body, weights)
        return weights

    for fetch in fetches[4:]:
        fetch.wait()
    cts[...] = fill(0, img_ref, ids_tx[2:3, :])

    pl.semaphore_wait(barrier, nz + ndp - 1)
    for piece in range(3):
        start_both(piece)
    ids_copy.start()
    img_copy.start()

    eye = lax.broadcasted_iota(I32, (pd, 2 * pd), 0) == lax.broadcasted_iota(I32, (pd, 2 * pd), 1)
    rot_col = jnp.sum(jnp.where(eye, ids_tx[1:2, :].astype(F32), 0.0), axis=1, keepdims=True)
    rot_hot = (lax.broadcasted_iota(I32, (pd, 64), 1).astype(F32) == rot_col).astype(F32)
    table = jnp.dot(rot_hot, tab_ref[...], precision=HIGHEST, preferred_element_type=F32)
    cosine, sine = table[:, :width], table[:, width:]
    tail[...] = jnp.zeros_like(tail)
    lane_p = lax.broadcasted_iota(I32, (1, 2 * pd), 1)
    tail[2 * kd : 2 * kd + 1, :] = jnp.where(lane_p < pd, ids_tx[0:1, :].astype(F32), 0.0)

    def turn_to(k, step, target):
        cycle = dp_peer(step) * kd + k
        row = xs[pl.ds(cycle, pd, stride=px), :]
        spun = row * cosine + pltpu.roll(row, modes, 1) * sine
        target[step, 16 + k * pd : 16 + (k + 1) * pd, :] = spun.astype(BF16)
        if k == 0:
            for at in range(kd):
                weight = cts[pl.ds(cycle + at, 1), :]
                square = jnp.where(lane_p < pd, weight * weight, 0.0)
                high = square.astype(BF16).astype(F32)
                tail[at : at + 1, :] = high
                tail[kd + at : kd + at + 1, :] = square - high
            target[step, 0:16, :] = tail[...].astype(BF16)

    def a2a(k, step):
        span = pl.ds(0, 16 + pd) if k == 0 else pl.ds(16 + k * pd, pd)
        return remote(
            a_tx.at[step, span], a_rx.at[step, span], aa_s.at[0], aa_r.at[k], (dp_peer(step), cls)
        )

    def a2a_all(k):
        span = pl.ds(0, 16 + pd) if k == 0 else pl.ds(16 + k * pd, pd)
        peers = pl.ds(1, ndp - 1)
        return remote(a_tx.at[peers, span], a_rx.at[peers, span], aa_s.at[0], aa_r.at[k], (dp_peer(1), cls))

    for k in range(kd):

        def send_turned(step, carry):
            turn_to(k, step, a_tx)
            a2a(k, step).start()
            return carry

        lax.fori_loop(1, ndp, send_turned, 0, unroll=5)
        turn_to(k, 0, a_rx)

    ids_copy.wait_recv()
    img_copy.wait_recv()
    fill(pd, img_rx, ids_rx[2:3, :])
    forward(1, 0)

    def flip(k, carry):
        s2[pl.ds(k * pk, width), :] = xs[pl.ds(k, 2 * pd, stride=px), :].T
        return carry

    lax.fori_loop(0, cy // 2, flip, 0, unroll=4)
    forward(1, 1)
    start_both(3)
    lax.fori_loop(cy // 2, cy, flip, 0, unroll=4)

    def spread(m, carry):
        re = s2[pl.ds(m, cy, stride=pk), :]
        im = s2[pl.ds(m + modes, cy, stride=pk), :]
        rhs[m, 0:cy, 0 : 2 * pd] = re.astype(BF16)
        rhs[m, 0:cy, 2 * pd : 4 * pd] = (-im).astype(BF16)
        rhs[m, cy : 2 * cy, 0 : 2 * pd] = im.astype(BF16)
        rhs[m, cy : 2 * cy, 2 * pd : 4 * pd] = re.astype(BF16)
        return carry

    lax.fori_loop(0, modes, spread, 0, unroll=4)

    lane2 = lax.broadcasted_iota(I32, (8, 2 * pd), 1)
    ids_all = jnp.where(lane2 < pd, ids_tx[...], pltpu.roll(ids_rx[...], pd, 1))
    class_row, rot_row = ids_all[0:1, :], ids_all[1:2, :]
    best_acc[...] = jnp.full_like(best_acc, -1e30)
    asg_acc[...] = jnp.zeros_like(asg_acc)
    sub8 = lax.broadcasted_iota(I32, (8, 2 * pd), 0)

    def score(first, count, between=None):
        high = count * cd

        def cross(m, carry):
            left = slots[first : first + count, m].reshape(high, 2 * cy)
            xm[m, 0:high, :] = jnp.dot(left, rhs[m], preferred_element_type=F32)
            return carry

        lax.fori_loop(0, modes, cross, 0, unroll=32)
        if between is not None:
            between()

        def column(col, carry):
            at = pl.multiple_of(col * 8, 8)
            slot = first + at // cd
            hop = (slot + 1) // 2
            source = (z + jnp.where(slot % 2 == 1, -hop, hop) + nz) % nz
            base = (source * CORES + core) * cd + at % cd
            re = lambda m: xm[m, pl.ds(at, 8), 0 : 2 * pd]
            im = lambda m: xm[m, pl.ds(at, 8), 2 * pd : 4 * pd]
            scores = rotation_scores(re, im, modes)
            top, chosen = None, jnp.zeros((8, 2 * pd), F32)
            for r, value in scores.items():
                top = value if top is None else jnp.maximum(top, value)
                chosen = jnp.where(rot_row == r, value, chosen)
            best_acc[...] = jnp.maximum(best_acc[...], top)
            asg_acc[...] = asg_acc[...] + jnp.where(class_row == base + sub8, chosen, 0.0)
            return carry

        lax.fori_loop(0, high // 8, column, 0)

    def one_hot():
        class_iota = lax.broadcasted_iota(I32, (ncls, 2 * pd), 0).astype(F32)
        for q in range(ndp // 2):
            near = a_rx[2 * q, 0:16, :].astype(F32)
            both = near + pltpu.roll(a_rx[2 * q + 1, 0:16, :].astype(F32), pd, 1)
            at = slice(q * 2 * pd, (q + 1) * 2 * pd)
            hot[:, at] = (class_iota == both[2 * kd : 2 * kd + 1, :]).astype(F32).astype(BF16)
            wrow[:, at] = both.astype(BF16)
        wacc[...] = jnp.zeros_like(wacc)
        wacc[:, 0:16] = lax.dot_general(hot[...], wrow[...], (((1,), (1,)), ((), ())), preferred_element_type=F32)

    def tiles(k):
        return 2 * cd if k == 0 else cd

    def at_class(owner):
        return pl.ds(pl.multiple_of(owner * cd, cd), cd)

    def with_rest(weights):
        high = weights.astype(BF16).astype(F32)
        return (high + pltpu.roll(weights - high, 16, 1)).astype(BF16)

    def without_rest(block):
        return block + pltpu.roll(block, width - 16, 1)

    def to_partner(k):
        span = pl.ds(0, tiles(k))
        return remote(p_tx.at[k, :, span], p_rx.at[k, :, span], pt_s.at[k], pt_r.at[k], partner)

    def to_owner(k, step):
        span = pl.ds(0, tiles(k))
        return remote(
            r_tx.at[k, step, span], r_rx.at[k, step, span], rs_s.at[k], rs_r.at[k], z_peer(step)
        )

    def to_owner_all(k):
        span, peers = pl.ds(0, tiles(k)), pl.ds(1, nz - 1)
        return remote(r_tx.at[k, peers, span], r_rx.at[k, peers, span], rs_s.at[k], rs_r.at[k], z_peer(1))

    def sum_cycle(k):
        a2a_all(k).wait_recv()
        if k == 0:
            one_hot()
        right = a_rx[:, 16 + k * pd : 16 + (k + 1) * pd, :].reshape(ndp * pd, width)
        facc[k] = jnp.dot(hot[...], right, preferred_element_type=F32)

        for chip in range(nz):
            at = at_class(chip * CORES + 1 - core)
            p_tx[k, chip, 0:cd, :] = facc[k, at, :].astype(BF16)
            if k == 0:
                p_tx[k, chip, cd : 2 * cd, :] = with_rest(wacc[at, :])
        to_partner(k).start()

    def chip_cycle(k):
        to_partner(k).wait_recv()

        def chip_sum(step):
            chip = (z + step) % nz
            at = at_class(chip * CORES + core)
            values = facc[k, at, :] + p_rx[k, chip, 0:cd, :].astype(F32)
            return values, (wacc[at, :] + without_rest(p_rx[k, chip, cd : 2 * cd, :].astype(F32)) if k == 0 else None)

        keep = lax.broadcasted_iota(I32, (cd, width), 1) < 16
        for step in range(1, nz):
            values, weights = chip_sum(step)
            r_tx[k, step, 0:cd, :] = values.astype(BF16)
            if k == 0:
                r_tx[k, step, cd : 2 * cd, :] = with_rest(jnp.where(keep, weights, 0.0))
        for step in sorted(range(1, nz), key=lambda step: -min(step, nz - step)):
            to_owner(k, step).start()
        values, weights = chip_sum(0)
        out_ref[k * cd : (k + 1) * cd, :] = values
        if k == 0:
            out_ref[kd * cd : (kd + 1) * cd, :] = weights

    def owned_cycle(k):
        to_owner_all(k).wait_recv()
        at = slice(k * cd, (k + 1) * cd)
        out_ref[at, :] = out_ref[at, :] + sum(r_rx[k, step, 0:cd, :].astype(F32) for step in range(1, nz))
        if k == 0:
            at = slice(kd * cd, (kd + 1) * cd)
            rest = sum(r_rx[k, step, cd : 2 * cd, :].astype(F32) for step in range(1, nz))
            out_ref[at, :] = out_ref[at, :] + without_rest(rest)

    todo = []
    for k in range(kd):
        todo.append((sum_cycle, k))
        if k > 0:
            todo.append((chip_cycle, k - 1))
    todo.append((chip_cycle, kd - 1))

    def some(count):
        for _ in range(min(count, len(todo))):
            act, k = todo.pop(0)
            act(k)

    some(1)
    for hop in range(2, hops - 1):
        forward(hop, 0)
        forward(hop, 1)
    for piece in (2, 3):
        for way in range(2):
            ag(way, 0, piece).wait_recv()
    last = hops - 1 if hops > 2 else None
    score(0, 3, last and (lambda: forward(last, 0)))
    if last:
        forward(last, 1)
    some(2)
    for slot in range(3, nz - 3, 2):
        complete(slot, slot + 1)
        score(slot, 2)
    forward_far(0)
    some(len(todo) - 1)
    forward_far(1)
    some(1)
    if last:
        complete(nz - 3, nz - 2)
        score(nz - 3, 2)
    complete(nz - 1)
    score(nz - 1, 1)

    e_tx[...] = jnp.zeros_like(e_tx)
    e_tx[0:1, :] = jnp.max(best_acc[...], axis=0, keepdims=True)
    e_tx[1:2, :] = jnp.sum(asg_acc[...], axis=0, keepdims=True)
    e_copy = remote(e_tx, e_rx, one_s.at[2], one_r.at[2], partner)
    e_copy.start()

    for k in range(kd):
        owned_cycle(k)

    e_copy.wait_recv()
    other = pltpu.roll(e_rx[...], pd, 1)
    low = (kd + 1) * cd
    out_ref[low : low + 1, :] = jnp.maximum(e_tx[0:1, :], other[0:1, :])
    out_ref[low + 1 : low + 2, :] = e_tx[1:2, :] + other[1:2, :]
    out_ref[low + 2 : low + 8, :] = jnp.zeros((6, width), F32)

    gone = slots.at[pl.ds(0, nz), pl.ds(0, quarter * (4 * hops + 2) // nz)]
    remote(gone, gone, ag_s.at[0], ag_r.at[0], z_peer(1)).wait_send()
    gone = slots.at[pl.ds(0, nz - 3), pl.ds(0, half)]
    remote(gone, gone, ag_s.at[1], ag_r.at[0], z_peer(1)).wait_send()
    gone = pl.ds(1, ndp - 1)
    remote(a_tx.at[gone], a_rx.at[gone], aa_s.at[0], aa_r.at[0], (dp_peer(1), cls)).wait_send()
    for k in range(kd):
        to_owner_all(k).wait_send()
        to_partner(k).wait_send()
    for copy in (img_copy, ids_copy, e_copy):
        copy.wait_send()


def deliver(pd, cd, kd, packed_ref, best_ref, asg_ref, sums_ref, wts_ref):
    low = (kd + 1) * cd
    best_ref[...] = packed_ref[low : low + 1, 0:pd]
    asg_ref[...] = packed_ref[low + 1 : low + 2, 0:pd]
    for k in range(kd):
        sums_ref[:, k, :] = packed_ref[k * cd : (k + 1) * cd, :]
    weights = packed_ref[kd * cd : (kd + 1) * cd, :].T
    wts_ref[...] = weights[0:kd, :] + weights[kd : 2 * kd, :]


def on_device(dims, images, references, ctf, class_ids, rot_ids, group_ids):
    ny, nx, nz, pd, cy, modes, cd = dims
    ndp, width, ncls = ny * nx, 2 * modes, nz * CORES * cd
    kd = cy // ndp
    hops = nz // 2
    block = kd * pd + 16
    most = 3 * cd
    row = lambda ids: ids.reshape(1, pd)
    vmem = pl.BlockSpec(memory_space=pltpu.VMEM)
    dma = pltpu.SemaphoreType.DMA
    packed = pl.pallas_call(
        functools.partial(kernel, dims),
        out_shape=jax.ShapeDtypeStruct(((kd + 1) * cd + 8, width), F32),
        in_specs=[pl.BlockSpec(memory_space=pl.ANY)] * 7,
        out_specs=vmem,
        scratch_shapes=[
            pltpu.VMEM((64, 2 * width), F32),
            pltpu.VMEM((pd, cy, width), BF16),
            pltpu.VMEM((cd, cy, width), BF16),
            pltpu.VMEM((cy, ctf.shape[0]), F32),
            pltpu.VMEM((1, pd), I32),
            pltpu.VMEM((1, pd), I32),
            pltpu.VMEM((1, pd), I32),
            pltpu.VMEM((pd, cy, width), BF16),
            pltpu.VMEM((8, 2 * pd), I32),
            pltpu.VMEM((8, 2 * pd), I32),
            pltpu.VMEM((2 * pd * (cy + 1), width), F32),
            pltpu.VMEM((cy * (width + 1), 2 * pd), F32),
            pltpu.VMEM((modes, 2 * cy, 4 * pd), BF16),
            pltpu.VMEM((cd * (modes + 1), 2 * cy), F32),
            pltpu.VMEM((nz, modes, cd, 2 * cy), BF16),
            pltpu.VMEM((modes, most, 4 * pd), F32),
            pltpu.VMEM((cy, 2 * pd), F32),
            pltpu.VMEM((16, 2 * pd), F32),
            pltpu.VMEM((ndp, block, width), BF16),
            pltpu.VMEM((ndp, block, width), BF16),
            pltpu.VMEM((ncls, ndp * pd), BF16),
            pltpu.VMEM((16, ndp * pd), BF16),
            pltpu.VMEM((kd, ncls, width), F32),
            pltpu.VMEM((ncls, width), F32),
            pltpu.VMEM((kd, nz, 2 * cd, width), BF16),
            pltpu.VMEM((kd, nz, 2 * cd, width), BF16),
            pltpu.VMEM((kd, nz, 2 * cd, width), BF16),
            pltpu.VMEM((kd, nz, 2 * cd, width), BF16),
            pltpu.VMEM((8, 2 * pd), F32),
            pltpu.VMEM((8, 2 * pd), F32),
            pltpu.VMEM((8, 2 * pd), F32),
            pltpu.VMEM((8, 2 * pd), F32),
            dma((2,)),
            dma((4 * hops + 4,)),
            dma((nz,)),
            dma((1,)),
            dma((kd,)),
            dma((kd,)),
            dma((kd,)),
            dma((kd,)),
            dma((kd,)),
            dma((3,)),
            dma((3,)),
            dma((7,)),
        ],
        compiler_params=pltpu.CompilerParams(
            collective_id=0, has_side_effects=True, vmem_limit_bytes=60 * 1024 * 1024
        ),
    )(
        jnp.asarray(turn_table(modes)), images, references, ctf.T, row(class_ids), row(rot_ids), row(group_ids)
    )
    best, assigned, sums, weights = pl.pallas_call(
        functools.partial(deliver, pd, cd, kd),
        out_shape=(
            jax.ShapeDtypeStruct((1, pd), F32),
            jax.ShapeDtypeStruct((1, pd), F32),
            jax.ShapeDtypeStruct((cd, kd, width), F32),
            jax.ShapeDtypeStruct((kd, cd), F32),
        ),
        in_specs=[vmem],
        out_specs=(vmem,) * 4,
    )(packed)
    return best.reshape(pd), assigned.reshape(pd), sums, weights.T


def plane(count):
    side = 1
    while side * side < count:
        side *= 2
    return count // side, side


def solution(mesh):
    ndp, ncl = mesh.shape["dp"], mesh.shape["cls"]
    ny, nx = plane(ndp)

    def step(images, references, ctf, class_ids, rot_ids, group_ids):
        pd, cy, width = images.shape
        dims = (ny, nx, ncl // CORES, pd, cy, width // 2, references.shape[0])
        return on_device(dims, images, references, ctf, class_ids, rot_ids, group_ids)

    both = P(("dp", "cls"))
    return jax.shard_map(
        step,
        mesh=mesh,
        in_specs=(P(("dp", "cls"), None, None), P("cls", None, None), P(), P(("dp", "cls"), None), both, both),
        out_specs=(both, both, P("cls", "dp", None), P("cls", "dp")),
        check_vma=False,
    )
```

```python
import functools
import math

import jax
import jax.numpy as jnp
import numpy as np
from jax import lax
from jax.experimental import pallas as pl
from jax.experimental.pallas import tpu as pltpu
from jax.sharding import PartitionSpec as P

ROT = 36
HALF = ROT // 2
QUART = ROT // 4
CORES = 2
F32 = jnp.float32
BF16 = jnp.bfloat16
I32 = jnp.int32
MESH = pl.DeviceIdType.MESH
HIGHEST = lax.Precision.HIGHEST


def bf16_value(x):
    return float(np.float32(x).astype(BF16))


def turn_table(modes):
    order = (np.arange(ROT)[:, None] * np.arange(modes)[None, :]) % ROT
    angle = order * (2.0 * math.pi / ROT)
    cos, sin = np.cos(angle), np.sin(angle)
    table = np.zeros((64, 4 * modes), np.float32)
    table[:ROT] = np.concatenate([cos, cos, -sin, sin], axis=1)
    return table


def weighted_sum(terms):
    groups = {}
    for coefficient, value in terms:
        size = round(abs(coefficient), 12)
        if size < 1e-9:
            continue
        groups.setdefault(size, []).append((coefficient > 0, value))
    total = None
    for size, members in groups.items():
        part = None
        for positive, value in members:
            if part is None:
                part = value if positive else -value
            else:
                part = part + value if positive else part - value
        if size != 1.0:
            part = part * F32(bf16_value(size))
        total = part if total is None else total + part
    return total


def rotation_scores(re, im, modes):
    fold_re, fold_im = [None] * ROT, [None] * ROT
    for m in range(modes):
        for fold, part in ((fold_re, re), (fold_im, im)):
            at = m % ROT
            fold[at] = part(m) if fold[at] is None else fold[at] + part(m)
    even = [None] * (HALF + 1)
    odd = [None] * (HALF + 1)
    even[0], even[HALF] = fold_re[0], fold_re[HALF]
    for m in range(1, HALF):
        even[m] = fold_re[m] + fold_re[ROT - m]
        odd[m] = fold_im[m] - fold_im[ROT - m]
    scores = {}
    for r in range(QUART + 1):
        cos = lambda m: math.cos(2.0 * math.pi * ((m * r) % ROT) / ROT)
        sin = lambda m: math.sin(2.0 * math.pi * ((m * r) % ROT) / ROT)
        ce = weighted_sum([(cos(m), even[m]) for m in range(0, HALF + 1, 2)])
        co = weighted_sum([(cos(m), even[m]) for m in range(1, HALF + 1, 2)])
        se = weighted_sum([(sin(m), odd[m]) for m in range(2, HALF, 2)])
        so = weighted_sum([(sin(m), odd[m]) for m in range(1, HALF, 2)])
        if r == 0:
            scores[0], scores[HALF] = ce + co, ce - co
        elif r == QUART:
            scores[r], scores[ROT - r] = ce - so, ce + so
        else:
            plus, minus, both, apart = ce + co, ce - co, se + so, se - so
            scores[r], scores[ROT - r] = plus - both, plus + both
            scores[HALF - r], scores[HALF + r] = minus + apart, minus - apart
    return scores


def kernel(
    dims,
    tab_hbm, img_hbm, refs_hbm, ctft_hbm, cid_hbm, rid_hbm, gid_hbm,
    out_ref,
    tab_ref, img_ref, refs_ref, ctft_ref, cid_ref, rid_ref, gid_ref,
    img_rx, ids_tx, ids_rx, xs, s2, rhs, s3, slots, xm, cts, tail, a_tx, a_rx,
    hot, wrow, facc, wacc, p_tx, p_rx, r_tx, r_rx, best_acc, asg_acc, e_tx, e_rx,
    ag_s, ag_r, sd_r, aa_s, aa_r, pt_s, pt_r, rs_s, rs_r, one_s, one_r, in_s,
):
    ny, nx, nz, pd, cy, modes, cd = dims
    ndp, width, ncls = ny * nx, 2 * modes, nz * CORES * cd
    kd = cy // ndp
    hops, half = nz // 2, modes // 2
    px, pk, pm = cy + 1, width + 1, modes + 1
    dp, cls = lax.axis_index("dp"), lax.axis_index("cls")
    z, core = cls // CORES, cls % CORES
    y, x = dp // nx, dp % nx
    partner = (dp, z * CORES + 1 - core)

    def z_peer(step):
        return (dp, ((z + step + nz) % nz) * CORES + core)

    def dp_peer(step):
        return ((y + step // nx) % ny) * nx + (x + step % nx) % nx

    def remote(src, dst, send, recv, device):
        return pltpu.make_async_remote_copy(
            src_ref=src, dst_ref=dst, send_sem=send, recv_sem=recv, device_id=device, device_id_type=MESH
        )

    fetches = []
    for at, (source, target) in enumerate((
        (refs_hbm, refs_ref), (cid_hbm, cid_ref), (rid_hbm, rid_ref), (gid_hbm, gid_ref),
        (ctft_hbm, ctft_ref), (tab_hbm, tab_ref), (img_hbm, img_ref),
    )):
        fetches.append(pltpu.make_async_copy(source, target, in_s.at[at]))
        fetches[-1].start()

    barrier = pltpu.get_barrier_semaphore()
    pl.semaphore_signal(barrier, inc=1, device_id=partner, device_id_type=MESH)
    for step in range(1, nz):
        pl.semaphore_signal(barrier, inc=1, device_id=z_peer(step), device_id_type=MESH)

    def greet(step, carry):
        pl.semaphore_signal(barrier, inc=1, device_id=(dp_peer(step), cls), device_id_type=MESH)
        return carry

    lax.fori_loop(1, ndp, greet, 0)

    for fetch in fetches[1:4]:
        fetch.wait()
    ids_tx[...] = jnp.zeros_like(ids_tx)
    ids_tx[0:1, 0:pd] = cid_ref[...]
    ids_tx[1:2, 0:pd] = rid_ref[...]
    ids_tx[2:3, 0:pd] = gid_ref[...]
    img_copy = remote(img_hbm, img_rx, one_s.at[0], one_r.at[0], partner)
    ids_copy = remote(ids_tx, ids_rx, one_s.at[1], one_r.at[1], partner)

    lane_k = lax.broadcasted_iota(I32, (modes, 2 * cy), 1)

    def ref_pair(p, carry):
        both = refs_ref[pl.ds(2 * p, 2)].astype(F32).reshape(2 * cy, width)
        turned = both.T
        re, im = turned[:modes], turned[modes:]
        s3[pl.ds(2 * p * pm, modes), :] = jnp.where(lane_k < cy, re, pltpu.roll(im, cy, 1))
        s3[pl.ds((2 * p + 1) * pm, modes), :] = jnp.where(
            lane_k < cy, pltpu.roll(re, cy, 1), im
        )
        return carry

    fetches[0].wait()
    lax.fori_loop(0, cd // 2, ref_pair, 0, unroll=4)

    color = (x + y) % 2
    quarter = modes // 4

    def slot_of(way, hop):
        return 0 if hop == 0 else nz - 1 if hop == hops else 2 * hop - 1 + way

    def piece_at(piece):
        return pl.ds(pl.multiple_of((color + piece // 2) % 2 * half + piece % 2 * quarter, quarter), quarter)

    def ag(way, hop, piece):
        at = 2 * piece + way if hop == 0 else 4 * (hop + 1) + 2 * piece + way
        return remote(
            slots.at[slot_of(way, hop), piece_at(piece)], slots.at[slot_of(way, hop + 1), piece_at(piece)],
            ag_s.at[0], ag_r.at[at], z_peer(1 - 2 * way),
        )

    def start_both(piece):
        for way in range(2):
            ag(way, 0, piece).start()

    def side(slot, axis):
        to = ((y + (ny - 1) * axis) % ny) * nx + (x + (nx - 1) * (1 - axis)) % nx
        ref = slots.at[slot, piece_at(axis)]
        return remote(ref, ref, ag_s.at[1], sd_r.at[slot], (to, cls))

    def complete(*wanted):
        for slot in wanted:
            ref = slots.at[slot, pl.ds(pl.multiple_of((color + 1) % 2 * half, half), half)]
            remote(ref, ref, ag_s.at[1], sd_r.at[slot], partner).wait_recv()

    def forward(hop, piece):
        for way in range(2):
            ag(way, hop - 1, piece).wait_recv()
            if hop < hops - 1 or piece == way:
                ag(way, hop, piece).start()
            if hop > 1:
                side(slot_of(way, hop), piece).start()

    def forward_far(way):
        ag(way, hops - 1, way).wait_recv()
        side(nz - 1, way).start()

    def ref_mode(m, carry):
        slots[0, m] = s3[pl.ds(m, cd, stride=pm), :].astype(BF16)
        return carry

    lax.fori_loop(0, modes, ref_mode, 0, unroll=8)

    def fill(base, image, groups):
        hot_g = (lax.broadcasted_iota(I32, (ctft_ref.shape[1], 2 * pd), 0) == groups).astype(F32)
        weights = jnp.dot(ctft_ref[...], hot_g, precision=HIGHEST, preferred_element_type=F32)

        def body(block, carry):
            for u in range(8):
                at = block * 8 + u
                xs[pl.ds((base + at) * px, cy), :] = image[at].astype(F32) * carry[:, u : u + 1]
            return pltpu.roll(carry, 2 * pd - 8, 1)

        lax.fori_loop(0, pd // 8, body, weights)
        return weights

    for fetch in fetches[4:]:
        fetch.wait()
    cts[...] = fill(0, img_ref, ids_tx[2:3, :])

    eye = lax.broadcasted_iota(I32, (pd, 2 * pd), 0) == lax.broadcasted_iota(I32, (pd, 2 * pd), 1)
    rot_col = jnp.sum(jnp.where(eye, ids_tx[1:2, :].astype(F32), 0.0), axis=1, keepdims=True)
    rot_hot = (lax.broadcasted_iota(I32, (pd, 64), 1).astype(F32) == rot_col).astype(F32)
    table = jnp.dot(rot_hot, tab_ref[...], precision=HIGHEST, preferred_element_type=F32)
    cosine, sine = table[:, :width], table[:, width:]
    tail[...] = jnp.zeros_like(tail)
    lane_p = lax.broadcasted_iota(I32, (1, 2 * pd), 1)
    tail[2 * kd : 2 * kd + 1, :] = jnp.where(lane_p < pd, ids_tx[0:1, :].astype(F32), 0.0)

    def turn_to(k, step, target):
        cycle = dp_peer(step) * kd + k
        row = xs[pl.ds(cycle, pd, stride=px), :]
        spun = row * cosine + pltpu.roll(row, modes, 1) * sine
        target[step, 16 + k * pd : 16 + (k + 1) * pd, :] = spun.astype(BF16)
        if k == 0:
            for at in range(kd):
                weight = cts[pl.ds(cycle + at, 1), :]
                square = jnp.where(lane_p < pd, weight * weight, 0.0)
                high = square.astype(BF16).astype(F32)
                tail[at : at + 1, :] = high
                tail[kd + at : kd + at + 1, :] = square - high
            target[step, 0:16, :] = tail[...].astype(BF16)

    def turn_first(step, carry):
        turn_to(0, step, a_tx)
        return carry

    lax.fori_loop(1, ndp, turn_first, 0, unroll=5)

    pl.semaphore_wait(barrier, nz + ndp - 1)
    for piece in range(3):
        start_both(piece)
    ids_copy.start()
    img_copy.start()

    def a2a(k, step):
        span = pl.ds(0, 16 + pd) if k == 0 else pl.ds(16 + k * pd, pd)
        return remote(
            a_tx.at[step, span], a_rx.at[step, span], aa_s.at[0], aa_r.at[k], (dp_peer(step), cls)
        )

    def a2a_all(k):
        span = pl.ds(0, 16 + pd) if k == 0 else pl.ds(16 + k * pd, pd)
        peers = pl.ds(1, ndp - 1)
        return remote(a_tx.at[peers, span], a_rx.at[peers, span], aa_s.at[0], aa_r.at[k], (dp_peer(1), cls))

    for k in range(kd):

        def send_turned(step, carry):
            if k > 0:
                turn_to(k, step, a_tx)
            a2a(k, step).start()
            return carry

        lax.fori_loop(1, ndp, send_turned, 0, unroll=5)
        turn_to(k, 0, a_rx)

    ids_copy.wait_recv()
    img_copy.wait_recv()
    fill(pd, img_rx, ids_rx[2:3, :])
    forward(1, 0)

    def flip(k, carry):
        s2[pl.ds(k * pk, width), :] = xs[pl.ds(k, 2 * pd, stride=px), :].T
        return carry

    lax.fori_loop(0, cy // 2, flip, 0, unroll=4)
    forward(1, 1)
    start_both(3)
    lax.fori_loop(cy // 2, cy, flip, 0, unroll=4)

    def spread(m, carry):
        re = s2[pl.ds(m, cy, stride=pk), :]
        im = s2[pl.ds(m + modes, cy, stride=pk), :]
        rhs[m, 0:cy, 0 : 2 * pd] = re.astype(BF16)
        rhs[m, 0:cy, 2 * pd : 4 * pd] = (-im).astype(BF16)
        rhs[m, cy : 2 * cy, 0 : 2 * pd] = im.astype(BF16)
        rhs[m, cy : 2 * cy, 2 * pd : 4 * pd] = re.astype(BF16)
        return carry

    lax.fori_loop(0, modes, spread, 0, unroll=4)

    lane2 = lax.broadcasted_iota(I32, (8, 2 * pd), 1)
    ids_all = jnp.where(lane2 < pd, ids_tx[...], pltpu.roll(ids_rx[...], pd, 1))
    class_row, rot_row = ids_all[0:1, :], ids_all[1:2, :]
    best_acc[...] = jnp.full_like(best_acc, -1e30)
    asg_acc[...] = jnp.zeros_like(asg_acc)
    sub8 = lax.broadcasted_iota(I32, (8, 2 * pd), 0)

    def score(first, count, between=None):
        high = count * cd

        def cross(m, carry):
            left = slots[first : first + count, m].reshape(high, 2 * cy)
            xm[m, 0:high, :] = jnp.dot(left, rhs[m], preferred_element_type=F32)
            return carry

        lax.fori_loop(0, modes, cross, 0, unroll=32)
        if between is not None:
            between()

        def column(col, carry):
            at = pl.multiple_of(col * 8, 8)
            slot = first + at // cd
            hop = (slot + 1) // 2
            source = (z + jnp.where(slot % 2 == 1, -hop, hop) + nz) % nz
            base = (source * CORES + core) * cd + at % cd
            re = lambda m: xm[m, pl.ds(at, 8), 0 : 2 * pd]
            im = lambda m: xm[m, pl.ds(at, 8), 2 * pd : 4 * pd]
            scores = rotation_scores(re, im, modes)
            top, chosen = None, jnp.zeros((8, 2 * pd), F32)
            for r, value in scores.items():
                top = value if top is None else jnp.maximum(top, value)
                chosen = jnp.where(rot_row == r, value, chosen)
            best_acc[...] = jnp.maximum(best_acc[...], top)
            asg_acc[...] = asg_acc[...] + jnp.where(class_row == base + sub8, chosen, 0.0)
            return carry

        lax.fori_loop(0, high // 8, column, 0)

    def one_hot():
        class_iota = lax.broadcasted_iota(I32, (ncls, 2 * pd), 0).astype(F32)
        for q in range(ndp // 2):
            near = a_rx[2 * q, 0:16, :].astype(F32)
            both = near + pltpu.roll(a_rx[2 * q + 1, 0:16, :].astype(F32), pd, 1)
            at = slice(q * 2 * pd, (q + 1) * 2 * pd)
            hot[:, at] = (class_iota == both[2 * kd : 2 * kd + 1, :]).astype(F32).astype(BF16)
            wrow[:, at] = both.astype(BF16)
        wacc[...] = jnp.zeros_like(wacc)
        wacc[:, 0:16] = lax.dot_general(hot[...], wrow[...], (((1,), (1,)), ((), ())), preferred_element_type=F32)

    def tiles(k):
        return 2 * cd if k == 0 else cd

    def at_class(owner):
        return pl.ds(pl.multiple_of(owner * cd, cd), cd)

    def with_rest(weights):
        high = weights.astype(BF16).astype(F32)
        return (high + pltpu.roll(weights - high, 16, 1)).astype(BF16)

    def without_rest(block):
        return block + pltpu.roll(block, width - 16, 1)

    def to_partner(k):
        span = pl.ds(0, tiles(k))
        return remote(p_tx.at[k, :, span], p_rx.at[k, :, span], pt_s.at[k], pt_r.at[k], partner)

    def to_owner(k, step):
        span = pl.ds(0, tiles(k))
        return remote(
            r_tx.at[k, step, span], r_rx.at[k, step, span], rs_s.at[k], rs_r.at[k], z_peer(step)
        )

    def to_owner_all(k):
        span, peers = pl.ds(0, tiles(k)), pl.ds(1, nz - 1)
        return remote(r_tx.at[k, peers, span], r_rx.at[k, peers, span], rs_s.at[k], rs_r.at[k], z_peer(1))

    def sum_cycle(k):
        a2a_all(k).wait_recv()
        if k == 0:
            one_hot()
        right = a_rx[:, 16 + k * pd : 16 + (k + 1) * pd, :].reshape(ndp * pd, width)
        facc[k] = jnp.dot(hot[...], right, preferred_element_type=F32)

        for chip in range(nz):
            at = at_class(chip * CORES + 1 - core)
            p_tx[k, chip, 0:cd, :] = facc[k, at, :].astype(BF16)
            if k == 0:
                p_tx[k, chip, cd : 2 * cd, :] = with_rest(wacc[at, :])
        to_partner(k).start()

    def chip_cycle(k):
        to_partner(k).wait_recv()

        def chip_sum(step):
            chip = (z + step) % nz
            at = at_class(chip * CORES + core)
            values = facc[k, at, :] + p_rx[k, chip, 0:cd, :].astype(F32)
            return values, (wacc[at, :] + without_rest(p_rx[k, chip, cd : 2 * cd, :].astype(F32)) if k == 0 else None)

        keep = lax.broadcasted_iota(I32, (cd, width), 1) < 16
        for step in range(1, nz):
            values, weights = chip_sum(step)
            r_tx[k, step, 0:cd, :] = values.astype(BF16)
            if k == 0:
                r_tx[k, step, cd : 2 * cd, :] = with_rest(jnp.where(keep, weights, 0.0))
        for step in sorted(range(1, nz), key=lambda step: -min(step, nz - step)):
            to_owner(k, step).start()
        values, weights = chip_sum(0)
        out_ref[k * cd : (k + 1) * cd, :] = values
        if k == 0:
            out_ref[kd * cd : (kd + 1) * cd, :] = weights

    def owned_cycle(k):
        to_owner_all(k).wait_recv()
        at = slice(k * cd, (k + 1) * cd)
        out_ref[at, :] = out_ref[at, :] + sum(r_rx[k, step, 0:cd, :].astype(F32) for step in range(1, nz))
        if k == 0:
            at = slice(kd * cd, (kd + 1) * cd)
            rest = sum(r_rx[k, step, cd : 2 * cd, :].astype(F32) for step in range(1, nz))
            out_ref[at, :] = out_ref[at, :] + without_rest(rest)

    todo = []
    for k in range(kd):
        todo.append((sum_cycle, k))
        if k > 0:
            todo.append((chip_cycle, k - 1))
    todo.append((chip_cycle, kd - 1))

    def some(count):
        for _ in range(min(count, len(todo))):
            act, k = todo.pop(0)
            act(k)

    some(1)
    for hop in range(2, hops - 1):
        forward(hop, 0)
        forward(hop, 1)
    for piece in (2, 3):
        for way in range(2):
            ag(way, 0, piece).wait_recv()
    last = hops - 1 if hops > 2 else None
    score(0, 3, last and (lambda: forward(last, 0)))
    if last:
        forward(last, 1)
    some(2)
    for slot in range(3, nz - 3, 2):
        complete(slot, slot + 1)
        score(slot, 2)
    forward_far(0)
    some(len(todo) - 1)
    forward_far(1)
    some(1)
    if last:
        complete(nz - 3, nz - 2)
        score(nz - 3, 2)
    complete(nz - 1)
    score(nz - 1, 1)

    e_tx[...] = jnp.zeros_like(e_tx)
    e_tx[0:1, :] = jnp.max(best_acc[...], axis=0, keepdims=True)
    e_tx[1:2, :] = jnp.sum(asg_acc[...], axis=0, keepdims=True)
    e_copy = remote(e_tx, e_rx, one_s.at[2], one_r.at[2], partner)
    e_copy.start()

    for k in range(kd):
        owned_cycle(k)

    e_copy.wait_recv()
    other = pltpu.roll(e_rx[...], pd, 1)
    low = (kd + 1) * cd
    out_ref[low : low + 1, :] = jnp.maximum(e_tx[0:1, :], other[0:1, :])
    out_ref[low + 1 : low + 2, :] = e_tx[1:2, :] + other[1:2, :]
    out_ref[low + 2 : low + 8, :] = jnp.zeros((6, width), F32)

    gone = slots.at[pl.ds(0, nz), pl.ds(0, quarter * (4 * hops + 2) // nz)]
    remote(gone, gone, ag_s.at[0], ag_r.at[0], z_peer(1)).wait_send()
    gone = slots.at[pl.ds(0, nz - 3), pl.ds(0, half)]
    remote(gone, gone, ag_s.at[1], ag_r.at[0], z_peer(1)).wait_send()
    gone = pl.ds(1, ndp - 1)
    remote(a_tx.at[gone], a_rx.at[gone], aa_s.at[0], aa_r.at[0], (dp_peer(1), cls)).wait_send()
    for k in range(kd):
        to_owner_all(k).wait_send()
        to_partner(k).wait_send()
    for copy in (img_copy, ids_copy, e_copy):
        copy.wait_send()


def deliver(pd, cd, kd, packed_ref, best_ref, asg_ref, sums_ref, wts_ref):
    low = (kd + 1) * cd
    best_ref[...] = packed_ref[low : low + 1, 0:pd]
    asg_ref[...] = packed_ref[low + 1 : low + 2, 0:pd]
    for k in range(kd):
        sums_ref[:, k, :] = packed_ref[k * cd : (k + 1) * cd, :]
    weights = packed_ref[kd * cd : (kd + 1) * cd, :].T
    wts_ref[...] = weights[0:kd, :] + weights[kd : 2 * kd, :]


def on_device(dims, images, references, ctf, class_ids, rot_ids, group_ids):
    ny, nx, nz, pd, cy, modes, cd = dims
    ndp, width, ncls = ny * nx, 2 * modes, nz * CORES * cd
    kd = cy // ndp
    hops = nz // 2
    block = kd * pd + 16
    most = 3 * cd
    row = lambda ids: ids.reshape(1, pd)
    vmem = pl.BlockSpec(memory_space=pltpu.VMEM)
    dma = pltpu.SemaphoreType.DMA
    packed = pl.pallas_call(
        functools.partial(kernel, dims),
        out_shape=jax.ShapeDtypeStruct(((kd + 1) * cd + 8, width), F32),
        in_specs=[pl.BlockSpec(memory_space=pl.ANY)] * 7,
        out_specs=vmem,
        scratch_shapes=[
            pltpu.VMEM((64, 2 * width), F32),
            pltpu.VMEM((pd, cy, width), BF16),
            pltpu.VMEM((cd, cy, width), BF16),
            pltpu.VMEM((cy, ctf.shape[0]), F32),
            pltpu.VMEM((1, pd), I32),
            pltpu.VMEM((1, pd), I32),
            pltpu.VMEM((1, pd), I32),
            pltpu.VMEM((pd, cy, width), BF16),
            pltpu.VMEM((8, 2 * pd), I32),
            pltpu.VMEM((8, 2 * pd), I32),
            pltpu.VMEM((2 * pd * (cy + 1) + cy, width), F32),
            pltpu.VMEM((cy * (width + 1) + width, 2 * pd), F32),
            pltpu.VMEM((modes, 2 * cy, 4 * pd), BF16),
            pltpu.VMEM((cd * (modes + 1) + modes, 2 * cy), F32),
            pltpu.VMEM((nz, modes, cd, 2 * cy), BF16),
            pltpu.VMEM((modes, most, 4 * pd), F32),
            pltpu.VMEM((cy, 2 * pd), F32),
            pltpu.VMEM((16, 2 * pd), F32),
            pltpu.VMEM((ndp, block, width), BF16),
            pltpu.VMEM((ndp, block, width), BF16),
            pltpu.VMEM((ncls, ndp * pd), BF16),
            pltpu.VMEM((16, ndp * pd), BF16),
            pltpu.VMEM((kd, ncls, width), F32),
            pltpu.VMEM((ncls, width), F32),
            pltpu.VMEM((kd, nz, 2 * cd, width), BF16),
            pltpu.VMEM((kd, nz, 2 * cd, width), BF16),
            pltpu.VMEM((kd, nz, 2 * cd, width), BF16),
            pltpu.VMEM((kd, nz, 2 * cd, width), BF16),
            pltpu.VMEM((8, 2 * pd), F32),
            pltpu.VMEM((8, 2 * pd), F32),
            pltpu.VMEM((8, 2 * pd), F32),
            pltpu.VMEM((8, 2 * pd), F32),
            dma((2,)),
            dma((4 * hops + 4,)),
            dma((nz,)),
            dma((1,)),
            dma((kd,)),
            dma((kd,)),
            dma((kd,)),
            dma((kd,)),
            dma((kd,)),
            dma((3,)),
            dma((3,)),
            dma((7,)),
        ],
        compiler_params=pltpu.CompilerParams(
            collective_id=0, has_side_effects=True, vmem_limit_bytes=60 * 1024 * 1024
        ),
    )(
        jnp.asarray(turn_table(modes)), images, references, ctf.T, row(class_ids), row(rot_ids), row(group_ids)
    )
    best, assigned, sums, weights = pl.pallas_call(
        functools.partial(deliver, pd, cd, kd),
        out_shape=(
            jax.ShapeDtypeStruct((1, pd), F32),
            jax.ShapeDtypeStruct((1, pd), F32),
            jax.ShapeDtypeStruct((cd, kd, width), F32),
            jax.ShapeDtypeStruct((kd, cd), F32),
        ),
        in_specs=[vmem],
        out_specs=(vmem,) * 4,
    )(packed)
    return best.reshape(pd), assigned.reshape(pd), sums, weights.T


def plane(count):
    side = 1
    while side * side < count:
        side *= 2
    return count // side, side


def solution(mesh):
    ndp, ncl = mesh.shape["dp"], mesh.shape["cls"]
    ny, nx = plane(ndp)

    def step(images, references, ctf, class_ids, rot_ids, group_ids):
        pd, cy, width = images.shape
        dims = (ny, nx, ncl // CORES, pd, cy, width // 2, references.shape[0])
        return on_device(dims, images, references, ctf, class_ids, rot_ids, group_ids)

    both = P(("dp", "cls"))
    return jax.shard_map(
        step,
        mesh=mesh,
        in_specs=(P(("dp", "cls"), None, None), P("cls", None, None), P(), P(("dp", "cls"), None), both, both),
        out_specs=(both, both, P("cls", "dp", None), P("cls", "dp")),
        check_vma=False,
    )
```
